512 devices in a mesh: lon: 32 (over z, core), lat: 16 (over y, x).
Axes of the slice: x: 4, y: 4, z: 16, core: 2. Of those that a mesh axis runs over, the one named last changes fastest.
Arguments:
- land_sea: int32 [2048, 7168], P('lat', 'lon'), may hold values from 0 to 1, as said below
- obs_cell: int32 [16, 32, 2048], P('lat', 'lon'), may hold values from 0 to 28671
- obs_value: float32 [16, 32, 2048], P('lat', 'lon'), may hold values from -12 to 12
- obs_weight: float32 [16, 32, 2048], P('lat', 'lon'), may hold values from 0.5 to 4
- intersection: int32 [16, 32], P('lat', 'lon'), may hold values from 1 to 16, as said below
- factors: float32 [160, 16, 16, 8192], P('lat', None, None, 'lon'), may hold values from -1 to 1, as said below
- coarse_inverse: float32 [8192, 8192], P(('lon', 'lat')), may hold values from -1 to 1, as said below
Outputs:
- solution: float32 [2048, 7168], P('lat', 'lon')
- residual: float32 [2048, 7168], P('lat', 'lon')
- preconditioned: float32 [2048, 7168], P('lat', 'lon')
The draws below stay inside these ranges and needn't reach their ends.
Inputs may be any that keep to these rules, and one draw needn't show every extreme that they name: `land_sea`: 1 marks ocean and 0 land; the first and last rows of the grid are land. Some tile has intersection 16. `factors`: each block is lower triangular (zero where the third index exceeds the second) with a positive diagonal. `coarse_inverse`: symmetric and positive definite.
All inputs are finite; a program needn't handle non-finite values.
Results may differ from the reference program's by a relative error of at most 0.00012.
Values sent between devices are 32-bit elements; how exact they have to be, the bound alone decides.
No kernel may reach another device: no remote copies, remote signals or barrier semaphores. Data moves between devices by JAX's collectives and lax.ppermute only.
A program may use at most 64 MiB of HBM per device.

```python
import math
import jax
import jax.numpy as jnp
from jax import lax

CY = 128
CX = 224
HW = 16
BS = 16
SUB = 4
OBS_DEV = 2048
ITERS = 1
LAT_TILES = 16
LON_TILES = 32
GRID_LAT = 2048
GRID_LON = 7168
LAT_EXT = 160
LON_EXT = 256
NBLK = 10
COARSE_ALL = 8192
N_LON = 32
N_LAT = 16


def draw_land_sea(key, part):
    key_block, key_cell = jax.random.split(jax.random.fold_in(key, 11))
    block_draw = jax.random.randint(key_block, (GRID_LAT // 4 + 1, GRID_LON // 4 + 1), 0, 100)
    block_land = jnp.repeat(jnp.repeat(block_draw < 28, 4, axis=0), 4, axis=1)[:GRID_LAT, :GRID_LON]
    cell_land = jax.random.randint(key_cell, (GRID_LAT, GRID_LON), 0, 100) < 6
    row_index = jnp.arange(GRID_LAT, dtype=jnp.int32)[:, None]
    polar = (row_index == 0) | (row_index == GRID_LAT - 1)
    land_cells = block_land | cell_land | polar
    return jnp.where(land_cells, 0, 1).astype(jnp.int32)


def draw_intersection(key, part):
    widths = jax.random.randint(jax.random.fold_in(key, 12), (LAT_TILES, LON_TILES), 1, HW + 1)
    first = (jnp.arange(LAT_TILES)[:, None] == 0) & (jnp.arange(LON_TILES)[None, :] == 0)
    return jnp.where(first, HW, widths).astype(jnp.int32)


def draw_obs_value(key, part):
    shape = (LAT_TILES, LON_TILES, OBS_DEV)
    lat_scale = 1.0 + 2.0 * jnp.arange(LAT_TILES, dtype=jnp.float32)[:, None, None] / max(LAT_TILES - 1, 1)
    lon_scale = 1.0 + 0.5 * jnp.arange(LON_TILES, dtype=jnp.float32)[None, :, None] / max(LON_TILES - 1, 1)
    inner_key = jax.random.fold_in(key, 13)
    base = jnp.clip(jax.random.normal(inner_key, shape, jnp.float32), -2.5, 2.5)
    return (base * lat_scale * lon_scale).astype(jnp.float32)


def draw_factors(key, part):
    shape = (LAT_TILES * NBLK, BS, BS, LON_TILES * LON_EXT)
    diag_shape = (LAT_TILES * NBLK, BS, 1, LON_TILES * LON_EXT)
    key_off, key_diag = jax.random.split(jax.random.fold_in(key, 14))
    off_diag = jnp.clip(0.12 * jax.random.normal(key_off, shape, jnp.float32), -0.3, 0.3)
    diagonal = jnp.exp(jax.random.uniform(key_diag, diag_shape, jnp.float32, math.log(0.3), math.log(0.8)))
    first_index = jnp.arange(BS)[:, None]
    second_index = jnp.arange(BS)[None, :]
    below = (second_index < first_index)[None, :, :, None]
    on_diag = (second_index == first_index)[None, :, :, None]
    return jnp.where(on_diag, diagonal, jnp.where(below, off_diag, 0.0)).astype(jnp.float32)


def draw_coarse_inverse(key, part):
    count = COARSE_ALL
    scale = 2.0 / (CY // SUB * (CX // SUB))
    key_noise, key_diag = jax.random.split(jax.random.fold_in(key, 15))
    noise = jnp.clip(jax.random.normal(key_noise, (count, count), jnp.float32), -5.0, 5.0)
    symmetric = (noise + noise.T) * (0.45 / math.sqrt(2.0 * count))
    diagonal = jnp.exp(jax.random.uniform(key_diag, (count,), jnp.float32, math.log(1.2), math.log(3.6)))
    return ((symmetric + jnp.diag(diagonal)) * scale).astype(jnp.float32)


def with_ends(entries, stream_key, smallest, high):
    longest = entries.shape.index(max(entries.shape))
    spots = []
    for shift in (0, 1):
        where = [jax.random.randint(jax.random.fold_in(stream_key, axis), (), 0, length) for axis, length in enumerate(entries.shape)]
        where[longest] = (where[longest] + shift) % entries.shape[longest]
        spots.append(tuple(where))
    return entries.at[spots[0]].set(smallest).at[spots[1]].set(high)


def steps_of(own_key, extent, cuts, least, top_value):
    gain, own = 1.0, jax.random.fold_in(own_key, 6)
    for position, shards_of in cuts:
        steps = jnp.exp(jax.random.uniform(jax.random.fold_in(own, position), (shards_of,), jnp.float32, least / len(cuts), top_value / len(cuts)))
        gain = gain * jnp.repeat(steps, extent[position] // shards_of).reshape([-1 if axis == position else 1 for axis in range(len(extent))])
    return gain


def setup_inputs(seed: int = 0) -> dict:
    streams_of = jax.random.split(jax.random.key(seed), 8)
    land_sea = draw_land_sea(jax.random.fold_in(streams_of[7], 71), 0)
    obs_cell = with_ends(jax.random.randint(streams_of[1], (LAT_TILES, LON_TILES, OBS_DEV), 0, CY * CX), jax.random.fold_in(streams_of[1], 1), 0, (CY * CX) - 1).astype(jnp.int32)
    obs_value = draw_obs_value(jax.random.fold_in(streams_of[7], 71), 0)
    obs_weight = jnp.clip(jnp.exp(math.log(4.0) - 2.0794415 * jax.random.uniform(streams_of[3], (LAT_TILES, LON_TILES, OBS_DEV), jnp.float32) ** steps_of(streams_of[3], (LAT_TILES, LON_TILES, OBS_DEV), ((0, 16), (1, 32)), -0.2, 0.2)), 0.5, 4.0)
    intersection = draw_intersection(jax.random.fold_in(streams_of[7], 71), 0)
    factors = draw_factors(jax.random.fold_in(streams_of[7], 71), 0)
    coarse_inverse = draw_coarse_inverse(jax.random.fold_in(streams_of[7], 71), 0)
    return dict(land_sea=land_sea, obs_cell=obs_cell, obs_value=obs_value, obs_weight=obs_weight, intersection=intersection, factors=factors, coarse_inverse=coarse_inverse)


DAMPING = 0.02


def wrap_pad(field, width):
    padded = jnp.pad(field, ((width, width), (0, 0)))
    return jnp.concatenate([padded[:, -width:], padded, padded[:, :width]], axis=1)


def tile_grid(per_tile):
    shaped = per_tile.reshape(N_LAT, N_LON, CY, CX)
    return jnp.transpose(shaped, (0, 2, 1, 3)).reshape(N_LAT * CY, N_LON * CX)


def operate(field, ocean, obs_diag, conduct):
    padded = wrap_pad(field, 1)
    east, west, north, south = conduct
    beside = east * padded[1:-1, 2:] + west * padded[1:-1, :-2] + north * padded[:-2, 1:-1] + south * padded[2:, 1:-1]
    coupling = (east + west + north + south) * field - beside
    return ocean * ((obs_diag + DAMPING) * field + coupling) + (1.0 - ocean) * field


def to_tiles(field):
    padded = wrap_pad(field, HW)
    upper = padded[:N_LAT * CY].reshape(N_LAT, CY, -1)[:, :2 * HW]
    lower = padded[2 * HW:].reshape(N_LAT, CY, -1)
    banded = jnp.concatenate([upper, lower], axis=1)
    left = banded[:, :, :N_LON * CX].reshape(N_LAT, LAT_EXT, N_LON, CX)[..., :2 * HW]
    right = banded[:, :, 2 * HW:].reshape(N_LAT, LAT_EXT, N_LON, CX)
    return jnp.concatenate([left, right], axis=3)


def from_tiles(contrib):
    upper = jnp.pad(contrib[:, :2 * HW], ((0, 0), (0, CY - 2 * HW), (0, 0), (0, 0)))
    upper = upper.reshape(N_LAT * CY, N_LON, LON_EXT)
    lower = contrib[:, 2 * HW:].reshape(N_LAT * CY, N_LON, LON_EXT)
    summed = jnp.pad(lower, ((2 * HW, 0), (0, 0), (0, 0))) + jnp.pad(upper, ((0, 2 * HW), (0, 0), (0, 0)))
    summed = summed[HW:HW + N_LAT * CY]
    left = jnp.pad(summed[..., :2 * HW], ((0, 0), (0, 0), (0, CX - 2 * HW))).reshape(N_LAT * CY, N_LON * CX)
    right = summed[..., 2 * HW:].reshape(N_LAT * CY, N_LON * CX)
    columns = jnp.pad(right, ((0, 0), (2 * HW, 0))) + jnp.pad(left, ((0, 0), (0, 2 * HW)))
    core = columns[:, HW:HW + N_LON * CX]
    wrapped_left = jnp.pad(columns[:, :HW], ((0, 0), (N_LON * CX - HW, 0)))
    wrapped_right = jnp.pad(columns[:, -HW:], ((0, 0), (0, N_LON * CX - HW)))
    return core + wrapped_left + wrapped_right


def reference(land_sea, obs_cell, obs_value, obs_weight, intersection, factors, coarse_inverse):
    ocean = land_sea.astype(jnp.float32)

    def cell_sums(cells, values):
        return jax.ops.segment_sum(values, cells, num_segments=CY * CX)

    obs_diag = tile_grid(jax.vmap(jax.vmap(cell_sums))(obs_cell, obs_weight))
    obs_load = tile_grid(jax.vmap(jax.vmap(cell_sums))(obs_cell, obs_weight * obs_value))
    rhs = ocean * obs_load

    ocean_pad = wrap_pad(ocean, 1)
    conduct = (ocean * ocean_pad[1:-1, 2:], ocean * ocean_pad[1:-1, :-2],
               ocean * ocean_pad[:-2, 1:-1], ocean * ocean_pad[2:, 1:-1])

    row_pos = jnp.arange(LAT_EXT, dtype=jnp.int32)
    col_pos = jnp.arange(LON_EXT, dtype=jnp.int32)
    reach = intersection.astype(jnp.int32)
    row_ok = (row_pos[None, :, None] >= HW - reach[:, None, :]) & (row_pos[None, :, None] < HW + CY + reach[:, None, :])
    col_ok = (col_pos[None, None, :] >= HW - reach[:, :, None]) & (col_pos[None, None, :] < HW + CX + reach[:, :, None])
    weights = to_tiles(ocean) * row_ok[..., None].astype(jnp.float32) * col_ok[:, None].astype(jnp.float32)
    blocks = factors.reshape(N_LAT, NBLK, BS, BS, N_LON * LON_EXT)

    def one_band(pair):
        band_factor, band_source = pair
        forward = jnp.einsum('kabx,kbx->kax', band_factor, band_source, precision=lax.Precision.HIGHEST)
        return jnp.einsum('kabx,kax->kbx', band_factor, forward, precision=lax.Precision.HIGHEST)

    def precondition(resid):
        source = (weights * to_tiles(resid)).reshape(N_LAT, NBLK, BS, N_LON * LON_EXT)
        solved = lax.map(one_band, (blocks, source))
        local = from_tiles(weights * solved.reshape(N_LAT, LAT_EXT, N_LON, LON_EXT))
        masked = (ocean * resid).reshape(N_LAT, SUB, CY // SUB, N_LON, SUB, CX // SUB)
        sums = jnp.sum(masked, axis=(2, 5))
        ordered = jnp.transpose(sums, (2, 0, 1, 3)).reshape(COARSE_ALL)
        answer = jnp.dot(coarse_inverse, ordered, precision=lax.Precision.HIGHEST, preferred_element_type=jnp.float32)
        placed = jnp.transpose(answer.reshape(N_LON, N_LAT, SUB, SUB), (1, 2, 0, 3))
        spread = jnp.broadcast_to(placed[:, :, None, :, :, None], (N_LAT, SUB, CY // SUB, N_LON, SUB, CX // SUB))
        return local + ocean * spread.reshape(N_LAT * CY, N_LON * CX)

    solution = jnp.zeros_like(rhs)
    residual = rhs
    precond = precondition(residual)
    first = precond
    affinity = jnp.sum(residual * precond)
    direction = precond
    for step in range(ITERS):
        image = operate(direction, ocean, obs_diag, conduct)
        alpha = affinity / jnp.sum(direction * image)
        solution = solution + alpha * direction
        residual = residual - alpha * image
        if step + 1 < ITERS:
            precond = precondition(residual)
            renewed = jnp.sum(residual * precond)
            direction = precond + (renewed / affinity) * direction
            affinity = renewed
    return solution, residual, first
```

```python
import jax
import jax.numpy as jnp
from jax import lax
from jax.experimental import pallas as pl
from jax.experimental.pallas import tpu as pltpu
from jax.sharding import PartitionSpec as P

F32 = jnp.float32
DAMPING = 0.02
ROWS, COLS, HW, EXT = 128, 224, 16, 256
BLK = 8
TRI = 192
QTR = TRI // 4
OBS = 2048

VM = pl.BlockSpec(memory_space=pltpu.VMEM)
SM = pl.BlockSpec(memory_space=pltpu.SMEM)


def iota(shape, dim):
    return lax.broadcasted_iota(jnp.int32, shape, dim)


def call(kernel, outs, ins, smem=0, scratch=(), flops=100000):
    size = sum(4 * x.size for x in ins)
    return pl.pallas_call(
        kernel,
        out_shape=[jax.ShapeDtypeStruct(s, F32) for s in outs],
        in_specs=[SM] * smem + [VM] * (len(ins) - smem),
        out_specs=[VM] * len(outs),
        scratch_shapes=list(scratch),
        cost_estimate=pl.CostEstimate(flops=flops, bytes_accessed=size, transcendentals=0),
    )(*ins)


def tri_rows(get):
    return jnp.concatenate([get(p, 8) for p in range(8)] + [get(p, 16) for p in range(8, 16)], axis=0)


def pack_kernel(reach_ref, fac_ref, east_ref, west_ref, south_ref, north_ref):
    reach = reach_ref[0, 0]
    lane = iota((TRI, 128), 1)
    row = iota((TRI, 128), 0)
    q = jnp.where(row < 64, row & 7, row & 15)
    first_rows = q >= HW - reach
    last_rows = q < reach
    east = jnp.zeros((TRI, 128), F32)
    west = jnp.zeros((TRI, 128), F32)
    for k in range(BLK):
        own = (lane >= k * 16) & (lane < k * 16 + 16)
        hi = tri_rows(lambda p, n: fac_ref[k + 1, p, 0:n, 128:256])
        lo = tri_rows(lambda p, n: fac_ref[k + 1, p, 0:n, 0:128])
        east = jnp.where(own & (lane - k * 16 < reach), pltpu.roll(hi, (k * 16 - 112) % 128, 1), east)
        west = jnp.where(own & (lane - k * 16 >= HW - reach), pltpu.roll(lo, k * 16, 1) if k else lo, west)
    east_ref[0:TRI, :] = east
    west_ref[0:TRI, :] = west
    top_lo = tri_rows(lambda p, n: fac_ref[0, p, 0:n, 0:128])
    top_hi = tri_rows(lambda p, n: fac_ref[0, p, 0:n, 128:256])
    end_lo = tri_rows(lambda p, n: fac_ref[BLK + 1, p, 0:n, 0:128])
    end_hi = tri_rows(lambda p, n: fac_ref[BLK + 1, p, 0:n, 128:256])
    top_lo = jnp.where(first_rows, top_lo, 0.0)
    top_hi = jnp.where(first_rows, top_hi, 0.0)
    end_lo = jnp.where(last_rows, end_lo, 0.0)
    end_hi = jnp.where(last_rows, end_hi, 0.0)
    east_corner = jnp.where(
        lane < 16, pltpu.roll(top_hi, 16, 1), jnp.where(lane < 32, pltpu.roll(end_hi, 32, 1), 0.0)
    )
    east_corner = jnp.where((lane & 15) < reach, east_corner, 0.0)
    west_corner = jnp.where(lane < 16, top_lo, jnp.where(lane < 32, pltpu.roll(end_lo, 16, 1), 0.0))
    west_corner = jnp.where((lane & 15) >= HW - reach, west_corner, 0.0)
    for ref, corner in ((east_ref, east_corner), (west_ref, west_corner)):
        packed = corner[0:QTR]
        for g in range(1, 4):
            packed = packed + pltpu.roll(corner[g * QTR : (g + 1) * QTR], 32 * g, 1)
        ref[TRI : TRI + QTR, :] = packed
    north_ref[:, 0:128] = jnp.where(lane >= 16, top_lo, 0.0)
    north_ref[:, 128:256] = jnp.where(lane < 112, top_hi, 0.0)
    south_ref[:, 0:128] = jnp.where(lane >= 16, end_lo, 0.0)
    south_ref[:, 128:256] = jnp.where(lane < 112, end_hi, 0.0)


def pieces(x):
    hi = x.astype(jnp.bfloat16).astype(F32)
    rest = x - hi
    mid = rest.astype(jnp.bfloat16).astype(F32)
    low = (rest - mid).astype(jnp.bfloat16).astype(F32)
    return hi, mid, low


def load_kernel(n_lat, lat_ref, cell_ref, value_ref, weight_ref, land_ref, diag_ref, rhs_ref, ocean_ref, send_ref,
                wide, left, right):
    me = lat_ref[0]
    wide[...] = jnp.zeros((ROWS, EXT), F32)
    wide[:, 0:COLS] = land_ref[...].astype(F32)
    ocean = pltpu.roll(wide[...], HW, 1)
    ocean_ref[...] = ocean
    step = 512
    for start in range(0, OBS, step):
        cut = slice(start, start + step)
        cell = cell_ref[:, cut]
        at_row = ((cell >> 5) * 9363) >> 16
        at_col = cell - at_row * COLS + HW
        weight = weight_ref[:, cut]
        parts = pieces(weight) + pieces(weight * value_ref[:, cut])
        hit = iota((ROWS, step), 0) == at_row
        for n, part in enumerate(parts):
            left[n * ROWS : (n + 1) * ROWS, cut] = jnp.where(hit, part, 0.0).astype(jnp.bfloat16)
        right[:, cut] = jnp.where(iota((EXT, step), 0) == at_col, 1.0, 0.0).astype(jnp.bfloat16)
    sums = lax.dot_general(left[...], right[...], (((1,), (1,)), ((), ())), preferred_element_type=F32)
    part = [sums[n * ROWS : (n + 1) * ROWS] for n in range(6)]
    diag_ref[...] = part[0] + (part[1] + part[2])
    rhs = ocean * (part[3] + (part[4] + part[5]))
    rhs_ref[...] = rhs
    sub = iota((16, EXT), 0)
    lane = iota((16, EXT), 1)
    pooled = jnp.zeros((16, EXT), F32)
    for s in range(4):
        band = jnp.sum(rhs[s * 32 : s * 32 + 32], axis=0, keepdims=True)
        pooled = jnp.where((sub >> 2) == s, band, pooled)
    first = HW + (sub & 3) * 56
    pooled = jnp.where((lane >= first) & (lane < first + 56), pooled, 0.0)
    coarse = jnp.sum(pooled, axis=1, keepdims=True)
    n_row = n_lat * 16 // 128
    placed = jnp.sum(jnp.where(lane == sub + 16 * me, coarse, 0.0), axis=0, keepdims=True)
    for p in range(n_lat):
        for r in range(n_row):
            send_ref[p, r : r + 1, :] = placed[:, r * 128 : (r + 1) * 128]
        face = jnp.where(p < me, ocean[0:1], ocean[ROWS - 1 : ROWS])
        send_ref[p, n_row : n_row + 1, :] = face[:, 0:128]
        send_ref[p, n_row + 1 : n_row + 2, :] = face[:, 128:256]


def merge_kernel(n_lon, n_row, from_w_ref, from_e_ref, south_ref, north_ref, got_ref, to_s_ref, to_n_ref, send_ref):
    lane = iota((QTR, 128), 1)
    for g in range(4):
        rows = slice(g * QTR, (g + 1) * QTR)
        packed_w = from_w_ref[TRI : TRI + QTR, :]
        packed_e = from_e_ref[TRI : TRI + QTR, :]
        for ref, base, shift in ((to_n_ref, north_ref, 0), (to_s_ref, south_ref, 16)):
            left = pltpu.roll(packed_w, (-32 * g - shift) % 128, 1) if g or shift else packed_w
            right = pltpu.roll(packed_e, (112 - 32 * g - shift) % 128, 1)
            ref[rows, 0:128] = jnp.where(lane < 16, left, base[rows, 0:128])
            ref[rows, 128:256] = jnp.where(lane >= 112, right, base[rows, 128:256])
    total = jnp.sum(got_ref[:, 0:n_row, :], axis=0)
    for p in range(n_lon):
        send_ref[p] = total


def apply_block(u, get):
    low = u[0:8]
    g_low = jnp.zeros_like(low)
    g_high = jnp.zeros_like(low)
    for p in range(8):
        line = get(p, 8)
        f = jnp.sum(line * low, axis=0, keepdims=True)
        g_low = g_low + line * f
    for p in range(8, 16):
        line = get(p, 16)
        f = jnp.sum(line * u, axis=0, keepdims=True)
        g = line * f
        g_low = g_low + g[0:8]
        g_high = g_high + g[8:16]
    return jnp.concatenate([g_low, g_high], axis=0)


def tri_get(ref):
    def get(p, n):
        start = p * 8 if p < 8 else 64 + (p - 8) * 16
        return ref[start : start + n, :]

    return get


def solve_kernel(n_lon, n_row, fac_ref, rhs_ref, ocean_ref, from_w_ref, from_e_ref, from_n_ref, from_s_ref,
                 inverse_ref, coarse_ref, z_ref, face_w_ref, face_e_ref, acc):
    lane = iota((16, 128), 1)
    wide_lane = iota((16, EXT), 1)
    u_w = jnp.zeros((16, 128), F32)
    u_e = jnp.zeros((16, 128), F32)
    for k in range(BLK):
        rows = slice(k * 16, k * 16 + 16)
        u = rhs_ref[rows, :]
        acc[rows, :] = apply_block(u, lambda p, n: fac_ref[k + 1, p, 0:n, :])
        own = (lane >= k * 16) & (lane < k * 16 + 16)
        u_w = jnp.where(own, pltpu.roll(u[:, 0:128], (k * 16 - 16) % 128, 1), u_w)
        u_e = jnp.where(own, pltpu.roll(u[:, 128:256], (k * 16 - 96) % 128, 1), u_e)
    g_w = apply_block(u_w, tri_get(from_w_ref))
    g_e = apply_block(u_e, tri_get(from_e_ref))
    for k in range(BLK):
        rows = slice(k * 16, k * 16 + 16)
        in_w = (lane >= 16) & (lane < 32)
        in_e = (lane >= 96) & (lane < 112)
        acc[rows, 0:128] += jnp.where(in_w, pltpu.roll(g_w, (16 - k * 16) % 128, 1), 0.0)
        acc[rows, 128:256] += jnp.where(in_e, pltpu.roll(g_e, (96 - k * 16) % 128, 1), 0.0)
    for rows, ref in ((slice(0, 16), from_n_ref), (slice(ROWS - 16, ROWS), from_s_ref)):
        u = rhs_ref[rows, :]
        u = jnp.where(
            wide_lane < 16, pltpu.roll(u, EXT - 16, 1), jnp.where(wide_lane >= 240, pltpu.roll(u, 16, 1), u)
        )
        g = apply_block(u, tri_get(ref))
        core = jnp.where((wide_lane >= 16) & (wide_lane < 240), g, 0.0)
        from_left = jnp.where((wide_lane >= 16) & (wide_lane < 32), pltpu.roll(g, 16, 1), 0.0)
        from_right = jnp.where((wide_lane >= 224) & (wide_lane < 240), pltpu.roll(g, EXT - 16, 1), 0.0)
        acc[rows, :] += core + from_left + from_right
    dot = jnp.zeros((16, 128), F32)
    for j in range(n_lon):
        for r in range(n_row):
            at = (j * n_row + r) * 128
            dot = dot + inverse_ref[:, at : at + 128] * coarse_ref[j, r : r + 1, :]
    answer = jnp.sum(dot, axis=1, keepdims=True)
    sub = iota((16, EXT), 0)
    first = HW + (sub & 3) * 56
    spread = jnp.where((wide_lane >= first) & (wide_lane < first + 56), answer, 0.0)
    for s in range(4):
        rows = slice(s * 32, s * 32 + 32)
        band = jnp.sum(jnp.where((sub >> 2) == s, spread, 0.0), axis=0, keepdims=True)
        z_ref[rows, :] = ocean_ref[rows, :] * (acc[rows, :] + band)
    z_left = jnp.transpose(z_ref[:, 0:128])
    z_right = jnp.transpose(z_ref[:, 128:256])
    o_left = jnp.transpose(ocean_ref[:, 0:128])
    o_right = jnp.transpose(ocean_ref[:, 128:256])
    face_w_ref[0:1, :] = z_left[16:17]
    face_w_ref[1:2, :] = o_left[16:17]
    face_e_ref[0:1, :] = z_right[111:112]
    face_e_ref[1:2, :] = o_right[111:112]


def image_kernel(n_lat, n_row, lat_ref, z_ref, ocean_ref, diag_ref, rhs_ref, got_ref, from_w_ref, from_e_ref,
                 image_ref, send_ref):
    me = lat_ref[0]
    lane = iota((ROWS, EXT), 1)
    row = iota((ROWS, EXT), 0)
    z = z_ref[...]
    ocean = ocean_ref[...]

    def column(ref, n):
        col = jnp.transpose(jnp.broadcast_to(ref[n : n + 1, :], (128, 128)))
        return jnp.concatenate([col, col], axis=1)

    def padded(x, n):
        return jnp.where(lane == 15, column(from_w_ref, n), jnp.where(lane == 240, column(from_e_ref, n), x))

    def sides(x):
        return pltpu.roll(x, 1, 1) + pltpu.roll(x, EXT - 1, 1)

    def line(index, inside):
        face = jnp.concatenate([got_ref[index, n_row : n_row + 1, :], got_ref[index, n_row + 1 : n_row + 2, :]], axis=1)
        return jnp.where(inside, face, 0.0)

    o_north = line(jnp.maximum(me - 1, 0), me > 0)
    o_south = line(jnp.minimum(me + 1, n_lat - 1), me < n_lat - 1)

    def rows(x, north, south):
        return jnp.where(row == 0, north, pltpu.roll(x, 1, 0)) + jnp.where(
            row == ROWS - 1, south, pltpu.roll(x, ROWS - 1, 0)
        )

    total = sides(padded(ocean, 1)) + rows(ocean, o_north, o_south)
    beside = sides(padded(z, 0)) + rows(z, 0.0, 0.0)
    image = ocean * ((diag_ref[...] + DAMPING) * z + (total * z - beside)) + (1.0 - ocean) * z
    image_ref[...] = image
    affinity = jnp.sum(jnp.sum(rhs_ref[...] * z, axis=0, keepdims=True), axis=1, keepdims=True)
    energy = jnp.sum(jnp.sum(z * image, axis=0, keepdims=True), axis=1, keepdims=True)
    small = iota((1, 128), 1)
    scalars = jnp.where(small == 0, affinity, jnp.where(small == 1, energy, 0.0))
    for p in range(n_lat):
        send_ref[p, 0:1, :] = z[0:1, 0:128]
        send_ref[p, 1:2, :] = z[0:1, 128:256]
        send_ref[p, 2:3, :] = z[ROWS - 1 : ROWS, 0:128]
        send_ref[p, 3:4, :] = z[ROWS - 1 : ROWS, 128:256]
        send_ref[p, 4:5, :] = scalars


def cross_kernel(n_lat, n_lon, got_ref, send_ref):
    cross = jnp.zeros((2, 128), F32)
    for i in range(n_lat - 1):
        cross = cross + got_ref[i, 2:4, :] * got_ref[i + 1, 0:2, :]
    cross = jnp.sum(jnp.sum(cross, axis=0, keepdims=True), axis=1, keepdims=True)
    small = iota((1, 128), 1)
    total = jnp.sum(got_ref[:, 4:5, :], axis=0) - jnp.where(small == 1, 2.0 * cross, 0.0)
    for p in range(n_lon):
        send_ref[p] = total


def final_kernel(n_lat, lat_ref, z_ref, image_ref, rhs_ref, ocean_ref, got_ref, sums_ref, sol_ref, res_ref, pre_ref):
    me = lat_ref[0]
    row = iota((ROWS, EXT), 0)
    z = z_ref[...]
    sums = jnp.sum(sums_ref[...], axis=0)
    small = iota((1, 128), 1)
    affinity = jnp.sum(jnp.where(small == 0, sums, 0.0), axis=1, keepdims=True)
    energy = jnp.sum(jnp.where(small == 1, sums, 0.0), axis=1, keepdims=True)
    alpha = affinity / energy

    def line(index, first, inside):
        face = jnp.concatenate([got_ref[index, first : first + 1, :], got_ref[index, first + 1 : first + 2, :]], axis=1)
        return jnp.where(inside, face, 0.0)

    z_north = line(jnp.maximum(me - 1, 0), 2, me > 0)
    z_south = line(jnp.minimum(me + 1, n_lat - 1), 0, me < n_lat - 1)
    edge = jnp.where(row == 0, z_north, jnp.where(row == ROWS - 1, z_south, 0.0))
    image = image_ref[...] - ocean_ref[...] * edge

    def store(ref, x):
        ref[...] = pltpu.roll(x, EXT - HW, 1)[:, 0:COLS]

    store(pre_ref, z)
    store(sol_ref, alpha * z)
    store(res_ref, rhs_ref[...] - alpha * image)


def body(land_sea, obs_cell, obs_value, obs_weight, intersection, factors, coarse_inverse):
    n_lat, n_lon = lax.axis_size("lat"), lax.axis_size("lon")
    n_row = n_lat * 16 // 128
    me = lax.axis_index("lat").astype(jnp.int32).reshape(1)
    ring = [(j, (j + 1) % n_lon) for j in range(n_lon)]
    back = [(b, a) for a, b in ring]
    line = [(i, i + 1) for i in range(n_lat - 1)]
    up = [(b, a) for a, b in line]
    tile = (ROWS, EXT)

    def k(kernel, *static):
        def run(*refs):
            kernel(*static, *refs)

        run.__name__ = kernel.__name__
        return run

    slab = (TRI + QTR, 128)
    to_e, to_w, south, north = call(
        pack_kernel, [slab, slab, (TRI, EXT), (TRI, EXT)], (intersection, factors), smem=1
    )
    from_w = lax.ppermute(to_e, "lon", ring)
    from_e = lax.ppermute(to_w, "lon", back)
    diag, rhs, ocean, send = call(
        k(load_kernel, n_lat),
        [tile, tile, tile, (n_lat, n_row + 2, 128)],
        (me, obs_cell.reshape(1, OBS), obs_value.reshape(1, OBS), obs_weight.reshape(1, OBS), land_sea),
        smem=1,
        scratch=[pltpu.VMEM(tile, F32), pltpu.VMEM((6 * ROWS, OBS), jnp.bfloat16), pltpu.VMEM((EXT, OBS), jnp.bfloat16)],
    )
    got = lax.all_to_all(send, "lat", 0, 0, tiled=True)
    to_s, to_n, send = call(
        k(merge_kernel, n_lon, n_row),
        [(TRI, EXT), (TRI, EXT), (n_lon, n_row, 128)],
        (from_w, from_e, south, north, got),
    )
    from_n = lax.ppermute(to_s, "lat", line)
    from_s = lax.ppermute(to_n, "lat", up)
    coarse = lax.all_to_all(send, "lon", 0, 0, tiled=True)
    z, face_w, face_e = call(
        k(solve_kernel, n_lon, n_row),
        [tile, (2, 128), (2, 128)],
        (factors, rhs, ocean, from_w, from_e, from_n, from_s, coarse_inverse, coarse),
        scratch=[pltpu.VMEM(tile, F32)],
    )
    z_w = lax.ppermute(face_e, "lon", ring)
    z_e = lax.ppermute(face_w, "lon", back)
    image, send = call(
        k(image_kernel, n_lat, n_row), [tile, (n_lat, 5, 128)], (me, z, ocean, diag, rhs, got, z_w, z_e), smem=1
    )
    edges = lax.all_to_all(send, "lat", 0, 0, tiled=True)
    (send,) = call(k(cross_kernel, n_lat, n_lon), [(n_lon, 1, 128)], (edges,))
    sums = lax.all_to_all(send, "lon", 0, 0, tiled=True)
    out = (ROWS, COLS)
    return tuple(
        call(k(final_kernel, n_lat), [out, out, out], (me, z, image, rhs, ocean, edges, sums), smem=1)
    )


def solution(mesh):
    in_specs = (
        P("lat", "lon"),
        P("lat", "lon", None),
        P("lat", "lon", None),
        P("lat", "lon", None),
        P("lat", "lon"),
        P("lat", None, None, "lon"),
        P(("lon", "lat"), None),
    )
    out_specs = (P("lat", "lon"), P("lat", "lon"), P("lat", "lon"))
    return jax.shard_map(body, mesh=mesh, in_specs=in_specs, out_specs=out_specs, check_vma=False)
```

```python
import jax
import jax.numpy as jnp
from jax import lax
from jax.experimental import pallas as pl
from jax.experimental.pallas import tpu as pltpu
from jax.sharding import PartitionSpec as P

F32 = jnp.float32
DAMPING = 0.02
ROWS, COLS, HW, EXT = 128, 224, 16, 256
BLK = 8
TRI = 192
OBS = 2048

VM = pl.BlockSpec(memory_space=pltpu.VMEM)
SM = pl.BlockSpec(memory_space=pltpu.SMEM)


def iota(shape, dim):
    return lax.broadcasted_iota(jnp.int32, shape, dim)


def call(kernel, outs, ins, smem=0, scratch=(), flops=100000, limit=16, hbm=0):
    size = sum(4 * x.size for x in ins)
    return pl.pallas_call(
        kernel,
        out_shape=[jax.ShapeDtypeStruct(s, F32) for s in outs],
        in_specs=[SM] * smem + [pl.BlockSpec(memory_space=pltpu.HBM)] * hbm + [VM] * (len(ins) - smem - hbm),
        out_specs=[VM] * len(outs),
        scratch_shapes=list(scratch),
        cost_estimate=pl.CostEstimate(flops=flops, bytes_accessed=size, transcendentals=0),
        compiler_params=pltpu.CompilerParams(vmem_limit_bytes=limit << 20),
    )(*ins)


def tri_rows(get):
    return jnp.concatenate([get(p, 8) for p in range(8)] + [get(p, 16) for p in range(8, 16)], axis=0)


def halo_kernel(reach_ref, fac_ref, south_ref, north_ref, first, last, sems):
    copies = [
        pltpu.make_async_copy(fac_ref.at[0], first, sems.at[0]),
        pltpu.make_async_copy(fac_ref.at[BLK + 1], last, sems.at[1]),
    ]
    for copy in copies:
        copy.start()
    reach = reach_ref[0, 0]
    lane = iota((TRI, EXT), 1)
    row = iota((TRI, EXT), 0)
    q = jnp.where(row < 64, row & 7, row & 15)
    inside = (lane >= HW - reach) & (lane < HW + COLS + reach)
    copies[0].wait()
    north_ref[...] = jnp.where(inside & (q >= HW - reach), tri_rows(lambda p, n: first[p, 0:n, :]), 0.0)
    copies[1].wait()
    south_ref[...] = jnp.where(inside & (q < reach), tri_rows(lambda p, n: last[p, 0:n, :]), 0.0)


def pieces(x):
    hi = x.astype(jnp.bfloat16).astype(F32)
    rest = x - hi
    mid = rest.astype(jnp.bfloat16).astype(F32)
    low = (rest - mid).astype(jnp.bfloat16).astype(F32)
    return hi, mid, low


def load_kernel(n_lat, lat_ref, cell_ref, value_ref, weight_ref, land_ref, diag_ref, rhs_ref, ocean_ref, send_ref,
                wide, left, right):
    me = lat_ref[0]
    wide[0:HW, :] = jnp.zeros((HW, ROWS), F32)
    wide[HW : HW + COLS, :] = land_ref[...].astype(F32)
    wide[HW + COLS : EXT, :] = jnp.zeros((HW, ROWS), F32)
    ocean = jnp.transpose(wide[...])
    ocean_ref[...] = ocean
    step = 512
    for start in range(0, OBS, step):
        cut = slice(start, start + step)
        cell = cell_ref[:, cut]
        at_row = ((cell >> 5) * 9363) >> 16
        at_col = cell - at_row * COLS + HW
        weight = weight_ref[:, cut]
        parts = pieces(weight) + pieces(weight * value_ref[:, cut])
        hit = iota((ROWS, step), 0) == at_row
        for n, part in enumerate(parts):
            left[n * ROWS : (n + 1) * ROWS, cut] = jnp.where(hit, part, 0.0).astype(jnp.bfloat16)
        right[:, cut] = jnp.where(iota((EXT, step), 0) == at_col, 1.0, 0.0).astype(jnp.bfloat16)
    sums = lax.dot_general(left[...], right[...], (((1,), (1,)), ((), ())), preferred_element_type=F32)
    part = [sums[n * ROWS : (n + 1) * ROWS] for n in range(6)]
    diag_ref[...] = part[0] + (part[1] + part[2])
    rhs = ocean * (part[3] + (part[4] + part[5]))
    rhs_ref[...] = rhs
    sub = iota((16, EXT), 0)
    lane = iota((16, EXT), 1)
    pooled = jnp.zeros((16, EXT), F32)
    for s in range(4):
        band = jnp.sum(rhs[s * 32 : s * 32 + 32], axis=0, keepdims=True)
        pooled = jnp.where((sub >> 2) == s, band, pooled)
    first = HW + (sub & 3) * 56
    pooled = jnp.where((lane >= first) & (lane < first + 56), pooled, 0.0)
    coarse = jnp.sum(pooled, axis=1, keepdims=True)
    n_row = n_lat * 16 // 128
    placed = jnp.sum(jnp.where(lane == sub + 16 * me, coarse, 0.0), axis=0, keepdims=True)
    for p in range(n_lat):
        for r in range(n_row):
            send_ref[p, r : r + 1, :] = placed[:, r * 128 : (r + 1) * 128]
        face = jnp.where(p < me, ocean[0:1], ocean[ROWS - 1 : ROWS])
        send_ref[p, n_row : n_row + 1, :] = face[:, 0:128]
        send_ref[p, n_row + 1 : n_row + 2, :] = face[:, 128:256]


def side_kernel(n_lon, n_row, reach_ref, fac_ref, from_n_ref, from_s_ref, got_ref, to_e_ref, to_w_ref, send_ref):
    reach = reach_ref[0, 0]
    lane = iota((TRI, 128), 1)
    east = jnp.zeros((TRI, 128), F32)
    west = jnp.zeros((TRI, 128), F32)
    for k in range(BLK):
        own = (lane >= k * 16) & (lane < k * 16 + 16)
        hi = tri_rows(lambda p, n: fac_ref[k + 1, p, 0:n, 128:256])
        lo = tri_rows(lambda p, n: fac_ref[k + 1, p, 0:n, 0:128])
        east = jnp.where(own & (lane - k * 16 < reach), pltpu.roll(hi, (k * 16 - 112) % 128, 1), east)
        west = jnp.where(own & (lane - k * 16 >= HW - reach), pltpu.roll(lo, k * 16, 1) if k else lo, west)
    to_e_ref[:, 0:128] = east
    to_w_ref[:, 0:128] = west
    north, south = from_n_ref[:, 128:256], from_s_ref[:, 128:256]
    to_e_ref[:, 128:256] = jnp.where(
        lane < 16, pltpu.roll(north, 16, 1), jnp.where(lane < 32, pltpu.roll(south, 32, 1), 0.0)
    )
    north, south = from_n_ref[:, 0:128], from_s_ref[:, 0:128]
    to_w_ref[:, 128:256] = jnp.where(lane < 16, north, jnp.where(lane < 32, pltpu.roll(south, 16, 1), 0.0))
    total = jnp.sum(got_ref[:, 0:n_row, :], axis=0)
    for p in range(n_lon):
        send_ref[p] = total


def apply_block(u, get):
    low = u[0:8]
    g_low = jnp.zeros_like(low)
    g_high = jnp.zeros_like(low)
    for p in range(8):
        line = get(p, 8)
        f = jnp.sum(line * low, axis=0, keepdims=True)
        g_low = g_low + line * f
    for p in range(8, 16):
        line = get(p, 16)
        f = jnp.sum(line * u, axis=0, keepdims=True)
        g = line * f
        g_low = g_low + g[0:8]
        g_high = g_high + g[8:16]
    return jnp.concatenate([g_low, g_high], axis=0)


def tri_get(ref):
    def get(p, n):
        start = p * 8 if p < 8 else 64 + (p - 8) * 16
        return ref[start : start + n, :]

    return get


def solve_kernel(n_lon, n_row, fac_ref, rhs_ref, ocean_ref, from_w_ref, from_e_ref, from_n_ref, from_s_ref,
                 inverse_ref, coarse_ref, z_ref, face_w_ref, face_e_ref, acc):
    lane = iota((16, 128), 1)
    wide_lane = iota((16, EXT), 1)
    u_w = jnp.zeros((16, 128), F32)
    u_e = jnp.zeros((16, 128), F32)
    for k in range(BLK):
        rows = slice(k * 16, k * 16 + 16)
        u = rhs_ref[rows, :]
        acc[rows, :] = apply_block(u, lambda p, n: fac_ref[k + 1, p, 0:n, :])
        own = (lane >= k * 16) & (lane < k * 16 + 16)
        u_w = jnp.where(own, pltpu.roll(u[:, 0:128], (k * 16 - 16) % 128, 1), u_w)
        u_e = jnp.where(own, pltpu.roll(u[:, 128:256], (k * 16 - 96) % 128, 1), u_e)
    top, end = rhs_ref[0:16, :], rhs_ref[ROWS - 16 : ROWS, :]

    def corners(top, end, at):
        return jnp.where(
            lane < 16, pltpu.roll(top, (-at) % 128, 1), jnp.where(lane < 32, pltpu.roll(end, (16 - at) % 128, 1), 0.0)
        )

    u_w = jnp.concatenate([u_w, corners(top[:, 0:128], end[:, 0:128], 16)], axis=1)
    u_e = jnp.concatenate([u_e, corners(top[:, 128:256], end[:, 128:256], 96)], axis=1)
    g_w = apply_block(u_w, tri_get(from_w_ref))
    g_e = apply_block(u_e, tri_get(from_e_ref))
    in_w = (lane >= 16) & (lane < 32)
    in_e = (lane >= 96) & (lane < 112)
    for k in range(BLK):
        rows = slice(k * 16, k * 16 + 16)
        add_w = pltpu.roll(g_w[:, 0:128], (16 - k * 16) % 128, 1)
        add_e = pltpu.roll(g_e[:, 0:128], (96 - k * 16) % 128, 1)
        if k == 0:
            add_w = add_w + pltpu.roll(g_w[:, 128:256], 16, 1)
            add_e = add_e + pltpu.roll(g_e[:, 128:256], 96, 1)
        if k == BLK - 1:
            add_w = add_w + g_w[:, 128:256]
            add_e = add_e + pltpu.roll(g_e[:, 128:256], 80, 1)
        acc[rows, 0:128] += jnp.where(in_w, add_w, 0.0)
        acc[rows, 128:256] += jnp.where(in_e, add_e, 0.0)
    for rows, ref in ((slice(0, 16), from_n_ref), (slice(ROWS - 16, ROWS), from_s_ref)):
        acc[rows, :] += apply_block(rhs_ref[rows, :], tri_get(ref))
    dot = jnp.zeros((16, 128), F32)
    for j in range(n_lon):
        for r in range(n_row):
            at = (j * n_row + r) * 128
            dot = dot + inverse_ref[:, at : at + 128] * coarse_ref[j, r : r + 1, :]
    answer = jnp.sum(dot, axis=1, keepdims=True)
    sub = iota((16, EXT), 0)
    first = HW + (sub & 3) * 56
    spread = jnp.where((wide_lane >= first) & (wide_lane < first + 56), answer, 0.0)
    for s in range(4):
        rows = slice(s * 32, s * 32 + 32)
        band = jnp.sum(jnp.where((sub >> 2) == s, spread, 0.0), axis=0, keepdims=True)
        z_ref[rows, :] = ocean_ref[rows, :] * (acc[rows, :] + band)
    z_left = jnp.transpose(z_ref[:, 0:128])
    z_right = jnp.transpose(z_ref[:, 128:256])
    o_left = jnp.transpose(ocean_ref[:, 0:128])
    o_right = jnp.transpose(ocean_ref[:, 128:256])
    face_w_ref[0:1, :] = z_left[16:17]
    face_w_ref[1:2, :] = o_left[16:17]
    face_e_ref[0:1, :] = z_right[111:112]
    face_e_ref[1:2, :] = o_right[111:112]


def image_kernel(n_lat, n_row, lat_ref, z_ref, ocean_ref, diag_ref, rhs_ref, got_ref, from_w_ref, from_e_ref,
                 image_ref, send_ref):
    me = lat_ref[0]
    lane = iota((ROWS, EXT), 1)
    row = iota((ROWS, EXT), 0)
    z = z_ref[...]
    ocean = ocean_ref[...]

    def column(ref, n):
        col = jnp.transpose(jnp.broadcast_to(ref[n : n + 1, :], (128, 128)))
        return jnp.concatenate([col, col], axis=1)

    def padded(x, n):
        return jnp.where(lane == 15, column(from_w_ref, n), jnp.where(lane == 240, column(from_e_ref, n), x))

    def sides(x):
        return pltpu.roll(x, 1, 1) + pltpu.roll(x, EXT - 1, 1)

    def line(index, inside):
        face = jnp.concatenate([got_ref[index, n_row : n_row + 1, :], got_ref[index, n_row + 1 : n_row + 2, :]], axis=1)
        return jnp.where(inside, face, 0.0)

    o_north = line(jnp.maximum(me - 1, 0), me > 0)
    o_south = line(jnp.minimum(me + 1, n_lat - 1), me < n_lat - 1)

    def rows(x, north, south):
        return jnp.where(row == 0, north, pltpu.roll(x, 1, 0)) + jnp.where(
            row == ROWS - 1, south, pltpu.roll(x, ROWS - 1, 0)
        )

    total = sides(padded(ocean, 1)) + rows(ocean, o_north, o_south)
    beside = sides(padded(z, 0)) + rows(z, 0.0, 0.0)
    image = ocean * ((diag_ref[...] + DAMPING) * z + (total * z - beside)) + (1.0 - ocean) * z
    image_ref[...] = image
    affinity = jnp.sum(jnp.sum(rhs_ref[...] * z, axis=0, keepdims=True), axis=1, keepdims=True)
    energy = jnp.sum(jnp.sum(z * image, axis=0, keepdims=True), axis=1, keepdims=True)
    small = iota((1, 128), 1)
    scalars = jnp.where(small == 0, affinity, jnp.where(small == 1, energy, 0.0))
    for p in range(n_lat):
        send_ref[p, 0:1, :] = z[0:1, 0:128]
        send_ref[p, 1:2, :] = z[0:1, 128:256]
        send_ref[p, 2:3, :] = z[ROWS - 1 : ROWS, 0:128]
        send_ref[p, 3:4, :] = z[ROWS - 1 : ROWS, 128:256]
        send_ref[p, 4:5, :] = scalars


def cross_kernel(n_lat, n_lon, got_ref, send_ref):
    cross = jnp.zeros((2, 128), F32)
    for i in range(n_lat - 1):
        cross = cross + got_ref[i, 2:4, :] * got_ref[i + 1, 0:2, :]
    cross = jnp.sum(jnp.sum(cross, axis=0, keepdims=True), axis=1, keepdims=True)
    small = iota((1, 128), 1)
    total = jnp.sum(got_ref[:, 4:5, :], axis=0) - jnp.where(small == 1, 2.0 * cross, 0.0)
    for p in range(n_lon):
        send_ref[p] = total


def final_kernel(n_lat, lat_ref, z_ref, image_ref, rhs_ref, ocean_ref, got_ref, sums_ref, sol_ref, res_ref, pre_ref):
    me = lat_ref[0]
    row = iota((ROWS, EXT), 0)
    z = z_ref[...]
    sums = jnp.sum(sums_ref[...], axis=0)
    small = iota((1, 128), 1)
    affinity = jnp.sum(jnp.where(small == 0, sums, 0.0), axis=1, keepdims=True)
    energy = jnp.sum(jnp.where(small == 1, sums, 0.0), axis=1, keepdims=True)
    alpha = affinity / energy

    def line(index, first, inside):
        face = jnp.concatenate([got_ref[index, first : first + 1, :], got_ref[index, first + 1 : first + 2, :]], axis=1)
        return jnp.where(inside, face, 0.0)

    z_north = line(jnp.maximum(me - 1, 0), 2, me > 0)
    z_south = line(jnp.minimum(me + 1, n_lat - 1), 0, me < n_lat - 1)
    edge = jnp.where(row == 0, z_north, jnp.where(row == ROWS - 1, z_south, 0.0))
    image = image_ref[...] - ocean_ref[...] * edge

    def store(ref, x):
        ref[...] = jnp.transpose(x)[HW : HW + COLS, :]

    store(pre_ref, z)
    store(sol_ref, alpha * z)
    store(res_ref, rhs_ref[...] - alpha * image)


def body(land_sea, obs_cell, obs_value, obs_weight, intersection, factors, coarse_inverse):
    n_lat, n_lon = lax.axis_size("lat"), lax.axis_size("lon")
    n_row = n_lat * 16 // 128
    me = lax.axis_index("lat").astype(jnp.int32).reshape(1)
    ring = [(j, (j + 1) % n_lon) for j in range(n_lon)]
    back = [(b, a) for a, b in ring]
    line = [(i, i + 1) for i in range(n_lat - 1)]
    up = [(b, a) for a, b in line]
    tile = (ROWS, EXT)

    def k(kernel, *static):
        def run(*refs):
            kernel(*static, *refs)

        run.__name__ = kernel.__name__
        return run

    slab = (TRI, EXT)
    to_s, to_n = call(
        halo_kernel,
        [slab, slab],
        (intersection, factors),
        smem=1,
        hbm=1,
        scratch=[pltpu.VMEM((16, 16, EXT), F32), pltpu.VMEM((16, 16, EXT), F32), pltpu.SemaphoreType.DMA((2,))],
    )
    from_n = lax.ppermute(to_s, "lat", line)
    from_s = lax.ppermute(to_n, "lat", up)
    diag, rhs, ocean, send = call(
        k(load_kernel, n_lat),
        [tile, tile, tile, (n_lat, n_row + 2, 128)],
        (me, obs_cell.reshape(1, OBS), obs_value.reshape(1, OBS), obs_weight.reshape(1, OBS), land_sea.T),
        smem=1,
        scratch=[pltpu.VMEM((EXT, ROWS), F32), pltpu.VMEM((6 * ROWS, OBS), jnp.bfloat16), pltpu.VMEM((EXT, OBS), jnp.bfloat16)],
    )
    got = lax.all_to_all(send, "lat", 0, 0, tiled=True)
    to_e, to_w, send = call(
        k(side_kernel, n_lon, n_row),
        [slab, slab, (n_lon, n_row, 128)],
        (intersection, factors, from_n, from_s, got),
        smem=1,
    )
    from_w = lax.ppermute(to_e, "lon", ring)
    from_e = lax.ppermute(to_w, "lon", back)
    coarse = lax.all_to_all(send, "lon", 0, 0, tiled=True)
    z, face_w, face_e = call(
        k(solve_kernel, n_lon, n_row),
        [tile, (2, 128), (2, 128)],
        (factors, rhs, ocean, from_w, from_e, from_n, from_s, coarse_inverse, coarse),
        scratch=[pltpu.VMEM(tile, F32)],
    )
    z_w = lax.ppermute(face_e, "lon", ring)
    z_e = lax.ppermute(face_w, "lon", back)
    image, send = call(
        k(image_kernel, n_lat, n_row), [tile, (n_lat, 5, 128)], (me, z, ocean, diag, rhs, got, z_w, z_e), smem=1
    )
    edges = lax.all_to_all(send, "lat", 0, 0, tiled=True)
    (send,) = call(k(cross_kernel, n_lat, n_lon), [(n_lon, 1, 128)], (edges,))
    sums = lax.all_to_all(send, "lon", 0, 0, tiled=True)
    out = (COLS, ROWS)
    return tuple(
        x.T for x in call(k(final_kernel, n_lat), [out, out, out], (me, z, image, rhs, ocean, edges, sums), smem=1)
    )


def solution(mesh):
    in_specs = (
        P("lat", "lon"),
        P("lat", "lon", None),
        P("lat", "lon", None),
        P("lat", "lon", None),
        P("lat", "lon"),
        P("lat", None, None, "lon"),
        P(("lon", "lat"), None),
    )
    out_specs = (P("lat", "lon"), P("lat", "lon"), P("lat", "lon"))
    return jax.shard_map(body, mesh=mesh, in_specs=in_specs, out_specs=out_specs, check_vma=False)
```

```python
import jax
import jax.numpy as jnp
from jax import lax
from jax.experimental import pallas as pl
from jax.experimental.pallas import tpu as pltpu
from jax.sharding import PartitionSpec as P

F32 = jnp.float32
DAMPING = 0.02
ROWS, COLS, HW, EXT = 128, 224, 16, 256
BLK = 8
TRI = 192
OBS = 2048

VM = pl.BlockSpec(memory_space=pltpu.VMEM)
PLACES = {
    "v": VM,
    "s": pl.BlockSpec(memory_space=pltpu.SMEM),
    "h": pl.BlockSpec(memory_space=pltpu.HBM),
}


def iota(shape, dim):
    return lax.broadcasted_iota(jnp.int32, shape, dim)


def call(kernel, outs, ins, scratch=(), flops=100000, limit=16384, places=None):
    size = sum(4 * x.size for x in ins)
    return pl.pallas_call(
        kernel,
        out_shape=[jax.ShapeDtypeStruct(s, F32) for s in outs],
        in_specs=[PLACES[p] for p in places or "v" * len(ins)],
        out_specs=[VM] * len(outs),
        scratch_shapes=list(scratch),
        cost_estimate=pl.CostEstimate(flops=flops, bytes_accessed=size, transcendentals=0),
        compiler_params=pltpu.CompilerParams(vmem_limit_bytes=limit << 10),
    )(*ins)


def tri_rows(get):
    return jnp.concatenate([get(p, 8) for p in range(8)] + [get(p, 16) for p in range(8, 16)], axis=0)


def pieces(x):
    hi = x.astype(jnp.bfloat16).astype(F32)
    rest = x - hi
    mid = rest.astype(jnp.bfloat16).astype(F32)
    low = (rest - mid).astype(jnp.bfloat16).astype(F32)
    return hi, mid, low


def first_kernel(n_lat, reach_ref, fac_hbm, land_hbm, cell_hbm, value_hbm, weight_hbm, south_ref, north_ref, diag_ref,
                 rhs_ref, ocean_ref, send_ref, first, last, wide, cell_ref, value_ref, weight_ref, left, right,
                 sems):
    moves = (
        (cell_hbm, cell_ref),
        (value_hbm, value_ref),
        (weight_hbm, weight_ref),
        (land_hbm, wide.at[pl.ds(HW, COLS), :]),
        (fac_hbm.at[0], first),
        (fac_hbm.at[BLK + 1], last),
    )
    copies = [pltpu.make_async_copy(src, dst, sems.at[n]) for n, (src, dst) in enumerate(moves)]
    for copy in copies:
        copy.start()
    me = lax.axis_index("lat")
    wide[0:HW, :] = jnp.zeros((HW, ROWS), jnp.int32)
    wide[HW + COLS : EXT, :] = jnp.zeros((HW, ROWS), jnp.int32)
    for copy in copies:
        copy.wait()
    edge = iota((TRI, EXT), 1)
    row = iota((TRI, EXT), 0)
    q = jnp.where(row < 64, row & 7, row & 15)
    reach = reach_ref[0, 0]
    inside = (edge >= HW - reach) & (edge < HW + COLS + reach)
    north_ref[...] = jnp.where(inside & (q >= HW - reach), tri_rows(lambda p, n: first[p, 0:n, :]), 0.0)
    south_ref[...] = jnp.where(inside & (q < reach), tri_rows(lambda p, n: last[p, 0:n, :]), 0.0)
    ocean = jnp.transpose(wide[...].astype(F32))
    ocean_ref[...] = ocean
    step = 512
    for start in range(0, OBS, step):
        cut = slice(start, start + step)
        cell = cell_ref[:, cut]
        at_row = ((cell >> 5) * 9363) >> 16
        at_col = cell - at_row * COLS + HW
        weight = weight_ref[:, cut]
        parts = pieces(weight) + pieces(weight * value_ref[:, cut])
        hit = iota((ROWS, step), 0) == at_row
        for n, part in enumerate(parts):
            left[n * ROWS : (n + 1) * ROWS, cut] = jnp.where(hit, part, 0.0).astype(jnp.bfloat16)
        right[:, cut] = jnp.where(iota((EXT, step), 0) == at_col, 1.0, 0.0).astype(jnp.bfloat16)
    sums = lax.dot_general(left[...], right[...], (((1,), (1,)), ((), ())), preferred_element_type=F32)
    part = [sums[n * ROWS : (n + 1) * ROWS] for n in range(6)]
    diag_ref[...] = part[0] + (part[1] + part[2])
    rhs = ocean * (part[3] + (part[4] + part[5]))
    rhs_ref[...] = rhs
    sub = iota((16, EXT), 0)
    lane = iota((16, EXT), 1)
    pooled = jnp.zeros((16, EXT), F32)
    for s in range(4):
        band = jnp.sum(rhs[s * 32 : s * 32 + 32], axis=0, keepdims=True)
        pooled = jnp.where((sub >> 2) == s, band, pooled)
    first = HW + (sub & 3) * 56
    pooled = jnp.where((lane >= first) & (lane < first + 56), pooled, 0.0)
    coarse = jnp.sum(pooled, axis=1, keepdims=True)
    n_row = n_lat * 16 // 128
    placed = jnp.sum(jnp.where(lane == sub + 16 * me, coarse, 0.0), axis=0, keepdims=True)
    for p in range(n_lat):
        for r in range(n_row):
            send_ref[p, r : r + 1, :] = placed[:, r * 128 : (r + 1) * 128]
        face = jnp.where(p < me, ocean[0:1], ocean[ROWS - 1 : ROWS])
        send_ref[p, n_row : n_row + 1, :] = face[:, 0:128]
        send_ref[p, n_row + 1 : n_row + 2, :] = face[:, 128:256]


def side_kernel(n_lon, n_row, reach_ref, fac_ref, from_n_ref, from_s_ref, got_ref, to_e_ref, to_w_ref, send_ref):
    reach = reach_ref[0, 0]
    lane = iota((TRI, 128), 1)
    east = jnp.zeros((TRI, 128), F32)
    west = jnp.zeros((TRI, 128), F32)
    for k in range(BLK):
        own = (lane >= k * 16) & (lane < k * 16 + 16)
        hi = tri_rows(lambda p, n: fac_ref[k + 1, p, 0:n, 128:256])
        lo = tri_rows(lambda p, n: fac_ref[k + 1, p, 0:n, 0:128])
        east = jnp.where(own & (lane - k * 16 < reach), pltpu.roll(hi, (k * 16 - 112) % 128, 1), east)
        west = jnp.where(own & (lane - k * 16 >= HW - reach), pltpu.roll(lo, k * 16, 1) if k else lo, west)
    to_e_ref[:, 0:128] = east
    to_w_ref[:, 0:128] = west
    north, south = from_n_ref[:, 128:256], from_s_ref[:, 128:256]
    to_e_ref[:, 128:256] = jnp.where(
        lane < 16, pltpu.roll(north, 16, 1), jnp.where(lane < 32, pltpu.roll(south, 32, 1), 0.0)
    )
    north, south = from_n_ref[:, 0:128], from_s_ref[:, 0:128]
    to_w_ref[:, 128:256] = jnp.where(lane < 16, north, jnp.where(lane < 32, pltpu.roll(south, 16, 1), 0.0))
    total = jnp.sum(got_ref[:, 0:n_row, :], axis=0)
    for p in range(n_lon):
        send_ref[p] = total


def apply_block(u, get):
    low = u[0:8]
    g_low = jnp.zeros_like(low)
    g_high = jnp.zeros_like(low)
    for p in range(8):
        line = get(p, 8)
        f = jnp.sum(line * low, axis=0, keepdims=True)
        g_low = g_low + line * f
    for p in range(8, 16):
        line = get(p, 16)
        f = jnp.sum(line * u, axis=0, keepdims=True)
        g = line * f
        g_low = g_low + g[0:8]
        g_high = g_high + g[8:16]
    return jnp.concatenate([g_low, g_high], axis=0)


def tri_get(ref):
    def get(p, n):
        start = p * 8 if p < 8 else 64 + (p - 8) * 16
        return ref[start : start + n, :]

    return get


def solve_kernel(n_lon, n_row, fac_ref, rhs_ref, ocean_ref, from_w_ref, from_e_ref, from_n_ref, from_s_ref,
                 inverse_ref, coarse_ref, z_ref, face_w_ref, face_e_ref, acc):
    lane = iota((16, 128), 1)
    wide_lane = iota((16, EXT), 1)
    u_w = jnp.zeros((16, 128), F32)
    u_e = jnp.zeros((16, 128), F32)
    for k in range(BLK):
        rows = slice(k * 16, k * 16 + 16)
        u = rhs_ref[rows, :]
        acc[rows, :] = apply_block(u, lambda p, n: fac_ref[k + 1, p, 0:n, :])
        own = (lane >= k * 16) & (lane < k * 16 + 16)
        u_w = jnp.where(own, pltpu.roll(u[:, 0:128], (k * 16 - 16) % 128, 1), u_w)
        u_e = jnp.where(own, pltpu.roll(u[:, 128:256], (k * 16 - 96) % 128, 1), u_e)
    top, end = rhs_ref[0:16, :], rhs_ref[ROWS - 16 : ROWS, :]

    def corners(top, end, at):
        return jnp.where(
            lane < 16, pltpu.roll(top, (-at) % 128, 1), jnp.where(lane < 32, pltpu.roll(end, (16 - at) % 128, 1), 0.0)
        )

    u_w = jnp.concatenate([u_w, corners(top[:, 0:128], end[:, 0:128], 16)], axis=1)
    u_e = jnp.concatenate([u_e, corners(top[:, 128:256], end[:, 128:256], 96)], axis=1)
    g_w = apply_block(u_w, tri_get(from_w_ref))
    g_e = apply_block(u_e, tri_get(from_e_ref))
    in_w = (lane >= 16) & (lane < 32)
    in_e = (lane >= 96) & (lane < 112)
    for k in range(BLK):
        rows = slice(k * 16, k * 16 + 16)
        add_w = pltpu.roll(g_w[:, 0:128], (16 - k * 16) % 128, 1)
        add_e = pltpu.roll(g_e[:, 0:128], (96 - k * 16) % 128, 1)
        if k == 0:
            add_w = add_w + pltpu.roll(g_w[:, 128:256], 16, 1)
            add_e = add_e + pltpu.roll(g_e[:, 128:256], 96, 1)
        if k == BLK - 1:
            add_w = add_w + g_w[:, 128:256]
            add_e = add_e + pltpu.roll(g_e[:, 128:256], 80, 1)
        acc[rows, 0:128] += jnp.where(in_w, add_w, 0.0)
        acc[rows, 128:256] += jnp.where(in_e, add_e, 0.0)
    for rows, ref in ((slice(0, 16), from_n_ref), (slice(ROWS - 16, ROWS), from_s_ref)):
        acc[rows, :] += apply_block(rhs_ref[rows, :], tri_get(ref))
    dot = jnp.zeros((16, 128), F32)
    for j in range(n_lon):
        for r in range(n_row):
            at = (j * n_row + r) * 128
            dot = dot + inverse_ref[:, at : at + 128] * coarse_ref[j, r : r + 1, :]
    answer = jnp.sum(dot, axis=1, keepdims=True)
    sub = iota((16, EXT), 0)
    first = HW + (sub & 3) * 56
    spread = jnp.where((wide_lane >= first) & (wide_lane < first + 56), answer, 0.0)
    for s in range(4):
        rows = slice(s * 32, s * 32 + 32)
        band = jnp.sum(jnp.where((sub >> 2) == s, spread, 0.0), axis=0, keepdims=True)
        z_ref[rows, :] = ocean_ref[rows, :] * (acc[rows, :] + band)
    z_left = jnp.transpose(z_ref[:, 0:128])
    z_right = jnp.transpose(z_ref[:, 128:256])
    o_left = jnp.transpose(ocean_ref[:, 0:128])
    o_right = jnp.transpose(ocean_ref[:, 128:256])
    face_w_ref[0:1, :] = z_left[16:17]
    face_w_ref[1:2, :] = o_left[16:17]
    face_e_ref[0:1, :] = z_right[111:112]
    face_e_ref[1:2, :] = o_right[111:112]


def image_kernel(n_lat, n_row, z_ref, ocean_ref, diag_ref, rhs_ref, got_ref, from_w_ref, from_e_ref,
                 image_ref, send_ref):
    me = lax.axis_index("lat")
    lane = iota((ROWS, EXT), 1)
    row = iota((ROWS, EXT), 0)
    z = z_ref[...]
    ocean = ocean_ref[...]

    def column(ref, n):
        col = jnp.transpose(jnp.broadcast_to(ref[n : n + 1, :], (128, 128)))
        return jnp.concatenate([col, col], axis=1)

    def padded(x, n):
        return jnp.where(lane == 15, column(from_w_ref, n), jnp.where(lane == 240, column(from_e_ref, n), x))

    def sides(x):
        return pltpu.roll(x, 1, 1) + pltpu.roll(x, EXT - 1, 1)

    def line(index, inside):
        face = jnp.concatenate([got_ref[index, n_row : n_row + 1, :], got_ref[index, n_row + 1 : n_row + 2, :]], axis=1)
        return jnp.where(inside, face, 0.0)

    o_north = line(jnp.maximum(me - 1, 0), me > 0)
    o_south = line(jnp.minimum(me + 1, n_lat - 1), me < n_lat - 1)

    def rows(x, north, south):
        return jnp.where(row == 0, north, pltpu.roll(x, 1, 0)) + jnp.where(
            row == ROWS - 1, south, pltpu.roll(x, ROWS - 1, 0)
        )

    total = sides(padded(ocean, 1)) + rows(ocean, o_north, o_south)
    beside = sides(padded(z, 0)) + rows(z, 0.0, 0.0)
    image = ocean * ((diag_ref[...] + DAMPING) * z + (total * z - beside)) + (1.0 - ocean) * z
    image_ref[...] = image
    affinity = jnp.sum(jnp.sum(rhs_ref[...] * z, axis=0, keepdims=True), axis=1, keepdims=True)
    energy = jnp.sum(jnp.sum(z * image, axis=0, keepdims=True), axis=1, keepdims=True)
    small = iota((1, 128), 1)
    scalars = jnp.where(small == 0, affinity, jnp.where(small == 1, energy, 0.0))
    for p in range(n_lat):
        send_ref[p, 0:1, :] = z[0:1, 0:128]
        send_ref[p, 1:2, :] = z[0:1, 128:256]
        send_ref[p, 2:3, :] = z[ROWS - 1 : ROWS, 0:128]
        send_ref[p, 3:4, :] = z[ROWS - 1 : ROWS, 128:256]
        send_ref[p, 4:5, :] = scalars


def cross_kernel(n_lat, n_lon, got_ref, send_ref):
    cross = jnp.zeros((2, 128), F32)
    for i in range(n_lat - 1):
        cross = cross + got_ref[i, 2:4, :] * got_ref[i + 1, 0:2, :]
    cross = jnp.sum(jnp.sum(cross, axis=0, keepdims=True), axis=1, keepdims=True)
    small = iota((1, 128), 1)
    total = jnp.sum(got_ref[:, 4:5, :], axis=0) - jnp.where(small == 1, 2.0 * cross, 0.0)
    for p in range(n_lon):
        send_ref[p] = total


def final_kernel(n_lat, z_ref, image_ref, rhs_ref, ocean_ref, got_ref, sums_ref, sol_ref, res_ref, pre_ref):
    me = lax.axis_index("lat")
    row = iota((ROWS, EXT), 0)
    z = z_ref[...]
    sums = jnp.sum(sums_ref[...], axis=0)
    small = iota((1, 128), 1)
    affinity = jnp.sum(jnp.where(small == 0, sums, 0.0), axis=1, keepdims=True)
    energy = jnp.sum(jnp.where(small == 1, sums, 0.0), axis=1, keepdims=True)
    alpha = affinity / energy

    def line(index, first, inside):
        face = jnp.concatenate([got_ref[index, first : first + 1, :], got_ref[index, first + 1 : first + 2, :]], axis=1)
        return jnp.where(inside, face, 0.0)

    z_north = line(jnp.maximum(me - 1, 0), 2, me > 0)
    z_south = line(jnp.minimum(me + 1, n_lat - 1), 0, me < n_lat - 1)
    edge = jnp.where(row == 0, z_north, jnp.where(row == ROWS - 1, z_south, 0.0))
    image = image_ref[...] - ocean_ref[...] * edge

    def store(ref, x):
        ref[...] = jnp.transpose(x)[HW : HW + COLS, :]

    store(pre_ref, z)
    store(sol_ref, alpha * z)
    store(res_ref, rhs_ref[...] - alpha * image)


def body(land_sea, obs_cell, obs_value, obs_weight, intersection, factors, coarse_inverse):
    n_lat, n_lon = lax.axis_size("lat"), lax.axis_size("lon")
    n_row = n_lat * 16 // 128
    ring = [(j, (j + 1) % n_lon) for j in range(n_lon)]
    back = [(b, a) for a, b in ring]
    line = [(i, i + 1) for i in range(n_lat - 1)]
    up = [(b, a) for a, b in line]
    tile = (ROWS, EXT)

    def k(kernel, *static):
        def run(*refs):
            kernel(*static, *refs)

        run.__name__ = kernel.__name__
        return run

    slab = (TRI, EXT)
    to_s, to_n, diag, rhs, ocean, send = call(
        k(first_kernel, n_lat),
        [slab, slab, tile, tile, tile, (n_lat, n_row + 2, 128)],
        (
            intersection,
            factors,
            land_sea.T,
            obs_cell.reshape(1, OBS),
            obs_value.reshape(1, OBS),
            obs_weight.reshape(1, OBS),
        ),
        places="shhhhh",
        limit=61000,
        scratch=[
            pltpu.VMEM((16, 16, EXT), F32),
            pltpu.VMEM((16, 16, EXT), F32),
            pltpu.VMEM((EXT, ROWS), jnp.int32),
            pltpu.VMEM((1, OBS), jnp.int32),
            pltpu.VMEM((1, OBS), F32),
            pltpu.VMEM((1, OBS), F32),
            pltpu.VMEM((6 * ROWS, OBS), jnp.bfloat16),
            pltpu.VMEM((EXT, OBS), jnp.bfloat16),
            pltpu.SemaphoreType.DMA((6,)),
        ],
    )
    from_n = lax.ppermute(to_s, "lat", line)
    from_s = lax.ppermute(to_n, "lat", up)
    got = lax.all_to_all(send, "lat", 0, 0, tiled=True)
    to_e, to_w, send = call(
        k(side_kernel, n_lon, n_row),
        [slab, slab, (n_lon, n_row, 128)],
        (intersection, factors, from_n, from_s, got),
        places="svvvv",
    )
    from_w = lax.ppermute(to_e, "lon", ring)
    from_e = lax.ppermute(to_w, "lon", back)
    coarse = lax.all_to_all(send, "lon", 0, 0, tiled=True)
    z, face_w, face_e = call(
        k(solve_kernel, n_lon, n_row),
        [tile, (2, 128), (2, 128)],
        (factors, rhs, ocean, from_w, from_e, from_n, from_s, coarse_inverse, coarse),
        scratch=[pltpu.VMEM(tile, F32)],
    )
    z_w = lax.ppermute(face_e, "lon", ring)
    z_e = lax.ppermute(face_w, "lon", back)
    image, send = call(
        k(image_kernel, n_lat, n_row), [tile, (n_lat, 5, 128)], (z, ocean, diag, rhs, got, z_w, z_e)
    )
    edges = lax.all_to_all(send, "lat", 0, 0, tiled=True)
    (send,) = call(k(cross_kernel, n_lat, n_lon), [(n_lon, 1, 128)], (edges,))
    sums = lax.all_to_all(send, "lon", 0, 0, tiled=True)
    out = (COLS, ROWS)
    return tuple(
        x.T for x in call(k(final_kernel, n_lat), [out, out, out], (z, image, rhs, ocean, edges, sums))
    )


def solution(mesh):
    in_specs = (
        P("lat", "lon"),
        P("lat", "lon", None),
        P("lat", "lon", None),
        P("lat", "lon", None),
        P("lat", "lon"),
        P("lat", None, None, "lon"),
        P(("lon", "lat"), None),
    )
    out_specs = (P("lat", "lon"), P("lat", "lon"), P("lat", "lon"))
    return jax.shard_map(body, mesh=mesh, in_specs=in_specs, out_specs=out_specs, check_vma=False)
```

```python
import jax
import jax.numpy as jnp
from jax import lax
from jax.experimental import pallas as pl
from jax.experimental.pallas import tpu as pltpu
from jax.sharding import PartitionSpec as P

F32 = jnp.float32
DAMPING = 0.02
ROWS, COLS, HW, EXT = 128, 224, 16, 256
BLK = 8
TRI = 192
OBS = 2048

VM = pl.BlockSpec(memory_space=pltpu.VMEM)
PLACES = {
    "v": VM,
    "s": pl.BlockSpec(memory_space=pltpu.SMEM),
    "h": pl.BlockSpec(memory_space=pltpu.HBM),
}


def iota(shape, dim):
    return lax.broadcasted_iota(jnp.int32, shape, dim)


def call(kernel, outs, ins, scratch=(), flops=100000, limit=16384, places=None):
    size = sum(4 * x.size for x in ins)
    return pl.pallas_call(
        kernel,
        out_shape=[jax.ShapeDtypeStruct(s, F32) for s in outs],
        in_specs=[PLACES[p] for p in places or "v" * len(ins)],
        out_specs=[VM] * len(outs),
        scratch_shapes=list(scratch),
        cost_estimate=pl.CostEstimate(flops=flops, bytes_accessed=size, transcendentals=0),
        compiler_params=pltpu.CompilerParams(vmem_limit_bytes=limit << 10),
    )(*ins)


def tri_rows(get):
    return jnp.concatenate([get(p, 8) for p in range(8)] + [get(p, 16) for p in range(8, 16)], axis=0)


def pieces(x):
    hi = x.astype(jnp.bfloat16).astype(F32)
    rest = x - hi
    mid = rest.astype(jnp.bfloat16).astype(F32)
    low = (rest - mid).astype(jnp.bfloat16).astype(F32)
    return hi, mid, low


def first_kernel(n_lat, reach_ref, fac_hbm, land_hbm, cell_hbm, value_hbm, weight_hbm, inverse_hbm, south_ref, north_ref, diag_ref,
                 rhs_ref, ocean_ref, send_ref, extra_ref, first, last, wide, cell_ref, value_ref, weight_ref, left, right,
                 inverse_ref, sems):
    moves = (
        (cell_hbm, cell_ref),
        (value_hbm, value_ref),
        (weight_hbm, weight_ref),
        (land_hbm, wide.at[pl.ds(HW, COLS), :]),
        (fac_hbm.at[0], first),
        (fac_hbm.at[BLK + 1], last),
        (inverse_hbm, inverse_ref),
    )
    copies = [pltpu.make_async_copy(src, dst, sems.at[n]) for n, (src, dst) in enumerate(moves)]
    for copy in copies:
        copy.start()
    me = lax.axis_index("lat")
    wide[0:HW, :] = jnp.zeros((HW, ROWS), jnp.int32)
    wide[HW + COLS : EXT, :] = jnp.zeros((HW, ROWS), jnp.int32)
    for copy in copies[:4]:
        copy.wait()
    ocean = jnp.transpose(wide[...].astype(F32))
    ocean_ref[...] = ocean
    step = 512
    for start in range(0, OBS, step):
        cut = slice(start, start + step)
        cell = cell_ref[:, cut]
        at_row = ((cell >> 5) * 9363) >> 16
        at_col = cell - at_row * COLS + HW
        weight = weight_ref[:, cut]
        parts = pieces(weight) + pieces(weight * value_ref[:, cut])
        hit = iota((ROWS, step), 0) == at_row
        for n, part in enumerate(parts):
            left[n * ROWS : (n + 1) * ROWS, cut] = jnp.where(hit, part, 0.0).astype(jnp.bfloat16)
        right[:, cut] = jnp.where(iota((EXT, step), 0) == at_col, 1.0, 0.0).astype(jnp.bfloat16)
    sums = lax.dot_general(left[...], right[...], (((1,), (1,)), ((), ())), preferred_element_type=F32)
    part = [sums[n * ROWS : (n + 1) * ROWS] for n in range(6)]
    diag_ref[...] = part[0] + (part[1] + part[2])
    rhs = ocean * (part[3] + (part[4] + part[5]))
    rhs_ref[...] = rhs
    sub = iota((16, EXT), 0)
    lane = iota((16, EXT), 1)
    pooled = jnp.zeros((16, EXT), F32)
    for s in range(4):
        band = jnp.sum(rhs[s * 32 : s * 32 + 32], axis=0, keepdims=True)
        pooled = jnp.where((sub >> 2) == s, band, pooled)
    begin = HW + (sub & 3) * 56
    pooled = jnp.where((lane >= begin) & (lane < begin + 56), pooled, 0.0)
    coarse = jnp.sum(pooled, axis=1, keepdims=True)
    n_row = n_lat * 16 // 128
    placed = jnp.sum(jnp.where(lane == sub + 16 * me, coarse, 0.0), axis=0, keepdims=True)
    for p in range(n_lat):
        for r in range(n_row):
            send_ref[p, r : r + 1, :] = placed[:, r * 128 : (r + 1) * 128]
        face = jnp.where(p < me, ocean[0:1], ocean[ROWS - 1 : ROWS])
        send_ref[p, n_row : n_row + 1, :] = face[:, 0:128]
        send_ref[p, n_row + 1 : n_row + 2, :] = face[:, 128:256]
    for copy in copies[4:6]:
        copy.wait()
    edge = iota((TRI, EXT), 1)
    row = iota((TRI, EXT), 0)
    q = jnp.where(row < 64, row & 7, row & 15)
    reach = reach_ref[0, 0]
    inside = (edge >= HW - reach) & (edge < HW + COLS + reach)
    north_ref[...] = jnp.where(inside & (q >= HW - reach), tri_rows(lambda p, n: first[p, 0:n, :]), 0.0)
    south_ref[...] = jnp.where(inside & (q < reach), tri_rows(lambda p, n: last[p, 0:n, :]), 0.0)
    side_lane = iota((16, EXT), 1)
    for half, face, edge in ((0, 16, 0), (1, 239, 15)):
        load = jnp.zeros((16, EXT), F32)
        mask = jnp.zeros((16, EXT), F32)
        for k in range(BLK):
            spots = (side_lane == k * 16 + edge) | (side_lane == 160 + k)
            if k == 0:
                spots = spots | (side_lane == 128 + edge) | (side_lane == 168)
            if k == BLK - 1:
                spots = spots | (side_lane == 144 + edge) | (side_lane == 169)
            load = jnp.where(spots, rhs[k * 16 : k * 16 + 16, face : face + 1], load)
            mask = jnp.where(spots, ocean[k * 16 : k * 16 + 16, face : face + 1], mask)
        extra_ref[half, 0:16, :] = load
        extra_ref[half, 16:32, :] = mask
    copies[6].wait()
    for half in range(2):
        for m in range(inverse_ref.shape[1] // EXT):
            for t in range(4):
                at_row, source = 32 + 4 * m + t, 4 * t + 3 * half
                extra_ref[half, at_row : at_row + 1, :] = inverse_ref[source : source + 1, m * EXT : (m + 1) * EXT]


def side_kernel(n_lon, n_row, reach_ref, fac_ref, from_n_ref, from_s_ref, extra_ref, got_ref, to_e_ref,
                to_w_ref, send_ref):
    reach = reach_ref[0, 0]
    lane = iota((TRI, 128), 1)
    for ref, half, face, start in ((to_e_ref, 1, 111, 112), (to_w_ref, 0, 16, 0)):
        lanes = slice(half * 128, half * 128 + 128)
        bulk = jnp.zeros((TRI, 128), F32)
        rest = jnp.zeros((TRI, 128), F32)
        for k in range(BLK):
            block = tri_rows(lambda p, n: fac_ref[k + 1, p, 0:n, lanes])
            at = lane - k * 16
            own = (at >= 0) & (at < jnp.minimum(reach, 16)) if half else (at >= HW - reach) & (at < 16)
            shift = (k * 16 - start) % 128
            bulk = jnp.where(own, pltpu.roll(block, shift, 1) if shift else block, bulk)
            rest = jnp.where(lane == 32 + k, pltpu.roll(block, (32 + k - face) % 128, 1), rest)
        north, south = from_n_ref[:, lanes], from_s_ref[:, lanes]
        rest = jnp.where(lane < 16, pltpu.roll(north, 16, 1) if half else north, rest)
        rest = jnp.where((lane >= 16) & (lane < 32), pltpu.roll(south, 32 if half else 16, 1), rest)
        rest = jnp.where(lane == 40, pltpu.roll(north, (40 - face) % 128, 1), rest)
        rest = jnp.where(lane == 41, pltpu.roll(south, (41 - face) % 128, 1), rest)
        ref[0:TRI, 0:128] = bulk
        ref[0:TRI, 128:256] = rest
        ref[TRI:, :] = extra_ref[half]
    total = jnp.sum(got_ref[:, 0:n_row, :], axis=0)
    for p in range(n_lon):
        send_ref[p] = total


def apply_block(u, get):
    low = u[0:8]
    g_low = jnp.zeros_like(low)
    g_high = jnp.zeros_like(low)
    for p in range(8):
        line = get(p, 8)
        f = jnp.sum(line * low, axis=0, keepdims=True)
        g_low = g_low + line * f
    for p in range(8, 16):
        line = get(p, 16)
        f = jnp.sum(line * u, axis=0, keepdims=True)
        g = line * f
        g_low = g_low + g[0:8]
        g_high = g_high + g[8:16]
    return jnp.concatenate([g_low, g_high], axis=0)


def tri_get(ref):
    def get(p, n):
        start = p * 8 if p < 8 else 64 + (p - 8) * 16
        return ref[start : start + n, :]

    return get


def solve_kernel(n_lat, n_lon, n_row, fac_ref, rhs_ref, ocean_ref, diag_ref, to_w_ref, to_e_ref, from_w_ref, from_e_ref,
                 from_n_ref, from_s_ref, inverse_ref, got_ref, coarse_ref, z_ref, image_ref, send_ref, acc, z_pad, o_pad):
    me = lax.axis_index("lat")
    lane = iota((16, 128), 1)
    wide_lane = iota((16, EXT), 1)
    u_w = jnp.zeros((16, 128), F32)
    u_e = jnp.zeros((16, 128), F32)
    for k in range(BLK):
        rows = slice(k * 16, k * 16 + 16)
        u = rhs_ref[rows, :]
        acc[rows, :] = apply_block(u, lambda p, n: fac_ref[k + 1, p, 0:n, :])
        own = (lane >= k * 16) & (lane < k * 16 + 16)
        u_w = jnp.where(own, pltpu.roll(u[:, 0:128], (k * 16 - 16) % 128, 1), u_w)
        u_e = jnp.where(own, pltpu.roll(u[:, 128:256], (k * 16 - 96) % 128, 1), u_e)
    top, end = rhs_ref[0:16, :], rhs_ref[ROWS - 16 : ROWS, :]

    def corners(top, end, at):
        return jnp.where(
            lane < 16, pltpu.roll(top, (-at) % 128, 1), jnp.where(lane < 32, pltpu.roll(end, (16 - at) % 128, 1), 0.0)
        )

    ring_w, ring_e = from_w_ref[TRI : TRI + 16, :], from_e_ref[TRI : TRI + 16, :]
    u_w = jnp.concatenate([u_w, corners(top[:, 0:128], end[:, 0:128], 16)], axis=1)
    u_e = jnp.concatenate([u_e, corners(top[:, 128:256], end[:, 128:256], 96)], axis=1)
    u_w = jnp.where(wide_lane >= 160, ring_w, u_w)
    u_e = jnp.where(wide_lane >= 160, ring_e, u_e)
    g_w = apply_block(u_w, tri_get(from_w_ref))
    g_e = apply_block(u_e, tri_get(from_e_ref))
    h_w = apply_block(ring_w, tri_get(to_w_ref))
    h_e = apply_block(ring_e, tri_get(to_e_ref))
    in_w = (lane >= 16) & (lane < 32)
    in_e = (lane >= 96) & (lane < 112)
    for k in range(BLK):
        rows = slice(k * 16, k * 16 + 16)
        add_w = pltpu.roll(g_w[:, 0:128], (16 - k * 16) % 128, 1)
        add_e = pltpu.roll(g_e[:, 0:128], (96 - k * 16) % 128, 1)
        if k == 0:
            add_w = add_w + pltpu.roll(g_w[:, 128:256], 16, 1)
            add_e = add_e + pltpu.roll(g_e[:, 128:256], 96, 1)
        if k == BLK - 1:
            add_w = add_w + g_w[:, 128:256]
            add_e = add_e + pltpu.roll(g_e[:, 128:256], 80, 1)
        acc[rows, 0:128] += jnp.where(in_w, add_w, 0.0)
        acc[rows, 128:256] += jnp.where(in_e, add_e, 0.0)
    for rows, ref in ((slice(0, 16), from_n_ref), (slice(ROWS - 16, ROWS), from_s_ref)):
        acc[rows, :] += apply_block(rhs_ref[rows, :], tri_get(ref))
    dot = jnp.zeros((16, EXT), F32)
    dot_w = jnp.zeros((4, EXT), F32)
    dot_e = jnp.zeros((4, EXT), F32)
    for m in range(n_lon * n_row // 2):
        part = [coarse_ref[n // n_row, n % n_row : n % n_row + 1, :] for n in (2 * m, 2 * m + 1)]
        part = jnp.concatenate(part, axis=1)
        dot = dot + inverse_ref[:, m * EXT : (m + 1) * EXT] * part
        at_row = TRI + 32 + 4 * m
        dot_w = dot_w + from_w_ref[at_row : at_row + 4, :] * part
        dot_e = dot_e + from_e_ref[at_row : at_row + 4, :] * part
    answer = jnp.sum(dot, axis=1, keepdims=True)
    answer_w = jnp.sum(dot_w, axis=1, keepdims=True)
    answer_e = jnp.sum(dot_e, axis=1, keepdims=True)
    sub = iota((16, EXT), 0)
    first = HW + (sub & 3) * 56
    spread = jnp.where((wide_lane >= first) & (wide_lane < first + 56), answer, 0.0)
    for k in range(BLK):
        rows = slice(k * 16, k * 16 + 16)
        s = k // 2
        band = jnp.sum(jnp.where((sub >> 2) == s, spread, 0.0), axis=0, keepdims=True)
        ocean = ocean_ref[rows, :]
        z = ocean * (acc[rows, :] + band)
        z_ref[rows, :] = z

        def edge(g, h, ref, at, answer):
            ring = h[:, k * 16 + at : k * 16 + at + 1] + g[:, 160 + k : 161 + k]
            if k == 0:
                ring = ring + (h[:, 128 + at : 129 + at] + g[:, 168:169])
            if k == BLK - 1:
                ring = ring + (h[:, 144 + at : 145 + at] + g[:, 169:170])
            mask = ref[TRI + 16 : TRI + 32, 160 + k : 161 + k]
            return mask, mask * (ring + answer[s : s + 1])

        o_w, z_w = edge(g_w, h_w, from_w_ref, 15, answer_w)
        o_e, z_e = edge(g_e, h_e, from_e_ref, 0, answer_e)
        z_pad[rows, :] = jnp.where(wide_lane == 15, z_w, jnp.where(wide_lane == 240, z_e, z))
        o_pad[rows, :] = jnp.where(wide_lane == 15, o_w, jnp.where(wide_lane == 240, o_e, ocean))

    row = iota((ROWS, EXT), 0)
    z = z_ref[...]
    ocean = ocean_ref[...]

    def sides(x):
        return pltpu.roll(x, 1, 1) + pltpu.roll(x, EXT - 1, 1)

    def line(index, inside):
        face = jnp.concatenate([got_ref[index, n_row : n_row + 1, :], got_ref[index, n_row + 1 : n_row + 2, :]], axis=1)
        return jnp.where(inside, face, 0.0)

    o_north = line(jnp.maximum(me - 1, 0), me > 0)
    o_south = line(jnp.minimum(me + 1, n_lat - 1), me < n_lat - 1)

    def rows(x, north, south):
        return jnp.where(row == 0, north, pltpu.roll(x, 1, 0)) + jnp.where(
            row == ROWS - 1, south, pltpu.roll(x, ROWS - 1, 0)
        )

    total = sides(o_pad[...]) + rows(ocean, o_north, o_south)
    beside = sides(z_pad[...]) + rows(z, 0.0, 0.0)
    image = ocean * ((diag_ref[...] + DAMPING) * z + (total * z - beside)) + (1.0 - ocean) * z
    image_ref[...] = image
    affinity = jnp.sum(jnp.sum(rhs_ref[...] * z, axis=0, keepdims=True), axis=1, keepdims=True)
    energy = jnp.sum(jnp.sum(z * image, axis=0, keepdims=True), axis=1, keepdims=True)
    small = iota((1, 128), 1)
    scalars = jnp.where(small == 0, affinity, jnp.where(small == 1, energy, 0.0))
    for p in range(n_lat):
        send_ref[p, 0:1, :] = z[0:1, 0:128]
        send_ref[p, 1:2, :] = z[0:1, 128:256]
        send_ref[p, 2:3, :] = z[ROWS - 1 : ROWS, 0:128]
        send_ref[p, 3:4, :] = z[ROWS - 1 : ROWS, 128:256]
        send_ref[p, 4:5, :] = scalars


def cross_kernel(n_lat, n_lon, got_ref, send_ref):
    cross = jnp.zeros((2, 128), F32)
    for i in range(n_lat - 1):
        cross = cross + got_ref[i, 2:4, :] * got_ref[i + 1, 0:2, :]
    cross = jnp.sum(jnp.sum(cross, axis=0, keepdims=True), axis=1, keepdims=True)
    small = iota((1, 128), 1)
    total = jnp.sum(got_ref[:, 4:5, :], axis=0) - jnp.where(small == 1, 2.0 * cross, 0.0)
    for p in range(n_lon):
        send_ref[p] = total


def final_kernel(n_lat, z_ref, image_ref, rhs_ref, ocean_ref, got_ref, sums_ref, sol_ref, res_ref, pre_ref):
    me = lax.axis_index("lat")
    row = iota((ROWS, EXT), 0)
    z = z_ref[...]
    sums = jnp.sum(sums_ref[...], axis=0)
    small = iota((1, 128), 1)
    affinity = jnp.sum(jnp.where(small == 0, sums, 0.0), axis=1, keepdims=True)
    energy = jnp.sum(jnp.where(small == 1, sums, 0.0), axis=1, keepdims=True)
    alpha = affinity / energy

    def line(index, first, inside):
        face = jnp.concatenate([got_ref[index, first : first + 1, :], got_ref[index, first + 1 : first + 2, :]], axis=1)
        return jnp.where(inside, face, 0.0)

    z_north = line(jnp.maximum(me - 1, 0), 2, me > 0)
    z_south = line(jnp.minimum(me + 1, n_lat - 1), 0, me < n_lat - 1)
    edge = jnp.where(row == 0, z_north, jnp.where(row == ROWS - 1, z_south, 0.0))
    image = image_ref[...] - ocean_ref[...] * edge

    def store(ref, x):
        ref[...] = jnp.transpose(x)[HW : HW + COLS, :]

    store(pre_ref, z)
    store(sol_ref, alpha * z)
    store(res_ref, rhs_ref[...] - alpha * image)


def body(land_sea, obs_cell, obs_value, obs_weight, intersection, factors, coarse_inverse):
    n_lat, n_lon = lax.axis_size("lat"), lax.axis_size("lon")
    n_row = n_lat * 16 // 128
    ring = [(j, (j + 1) % n_lon) for j in range(n_lon)]
    back = [(b, a) for a, b in ring]
    line = [(i, i + 1) for i in range(n_lat - 1)]
    up = [(b, a) for a, b in line]
    tile = (ROWS, EXT)

    def k(kernel, *static):
        def run(*refs):
            kernel(*static, *refs)

        run.__name__ = kernel.__name__
        return run

    slab = (TRI, EXT)
    more = 32 + 4 * coarse_inverse.shape[1] // EXT
    to_s, to_n, diag, rhs, ocean, send, extra = call(
        k(first_kernel, n_lat),
        [slab, slab, tile, tile, tile, (n_lat, n_row + 2, 128), (2, more, EXT)],
        (
            intersection,
            factors,
            land_sea.T,
            obs_cell.reshape(1, OBS),
            obs_value.reshape(1, OBS),
            obs_weight.reshape(1, OBS),
            coarse_inverse,
        ),
        places="shhhhhh",
        limit=61000,
        scratch=[
            pltpu.VMEM((16, 16, EXT), F32),
            pltpu.VMEM((16, 16, EXT), F32),
            pltpu.VMEM((EXT, ROWS), jnp.int32),
            pltpu.VMEM((1, OBS), jnp.int32),
            pltpu.VMEM((1, OBS), F32),
            pltpu.VMEM((1, OBS), F32),
            pltpu.VMEM((6 * ROWS, OBS), jnp.bfloat16),
            pltpu.VMEM((EXT, OBS), jnp.bfloat16),
            pltpu.VMEM(coarse_inverse.shape, F32),
            pltpu.SemaphoreType.DMA((7,)),
        ],
    )
    from_n = lax.ppermute(to_s, "lat", line)
    from_s = lax.ppermute(to_n, "lat", up)
    got = lax.all_to_all(send, "lat", 0, 0, tiled=True)
    message = (TRI + more, EXT)
    to_e, to_w, send = call(
        k(side_kernel, n_lon, n_row),
        [message, message, (n_lon, n_row, 128)],
        (intersection, factors, from_n, from_s, extra, got),
        places="svvvvv",
    )
    from_w = lax.ppermute(to_e, "lon", ring)
    from_e = lax.ppermute(to_w, "lon", back)
    coarse = lax.all_to_all(send, "lon", 0, 0, tiled=True)
    z, image, send = call(
        k(solve_kernel, n_lat, n_lon, n_row),
        [tile, tile, (n_lat, 5, 128)],
        (factors, rhs, ocean, diag, to_w, to_e, from_w, from_e, from_n, from_s, coarse_inverse, got, coarse),
        scratch=[pltpu.VMEM(tile, F32), pltpu.VMEM(tile, F32), pltpu.VMEM(tile, F32)],
    )
    edges = lax.all_to_all(send, "lat", 0, 0, tiled=True)
    (send,) = call(k(cross_kernel, n_lat, n_lon), [(n_lon, 1, 128)], (edges,))
    sums = lax.all_to_all(send, "lon", 0, 0, tiled=True)
    out = (COLS, ROWS)
    return tuple(
        x.T for x in call(k(final_kernel, n_lat), [out, out, out], (z, image, rhs, ocean, edges, sums))
    )


def solution(mesh):
    in_specs = (
        P("lat", "lon"),
        P("lat", "lon", None),
        P("lat", "lon", None),
        P("lat", "lon", None),
        P("lat", "lon"),
        P("lat", None, None, "lon"),
        P(("lon", "lat"), None),
    )
    out_specs = (P("lat", "lon"), P("lat", "lon"), P("lat", "lon"))
    return jax.shard_map(body, mesh=mesh, in_specs=in_specs, out_specs=out_specs, check_vma=False)
```

```python
import jax
import jax.numpy as jnp
from jax import lax
from jax.experimental import pallas as pl
from jax.experimental.pallas import tpu as pltpu
from jax.sharding import PartitionSpec as P

F32 = jnp.float32
DAMPING = 0.02
ROWS, COLS, HW, EXT = 128, 224, 16, 256
BLK = 8
TRI = 192
OBS = 2048

VM = pl.BlockSpec(memory_space=pltpu.VMEM)
PLACES = {
    "v": VM,
    "s": pl.BlockSpec(memory_space=pltpu.SMEM),
    "h": pl.BlockSpec(memory_space=pltpu.HBM),
}


def iota(shape, dim):
    return lax.broadcasted_iota(jnp.int32, shape, dim)


def call(kernel, outs, ins, scratch=(), flops=100000, limit=16384, places=None):
    size = sum(4 * x.size for x in ins)
    return pl.pallas_call(
        kernel,
        out_shape=[jax.ShapeDtypeStruct(s, F32) for s in outs],
        in_specs=[PLACES[p] for p in places or "v" * len(ins)],
        out_specs=[VM] * len(outs),
        scratch_shapes=list(scratch),
        cost_estimate=pl.CostEstimate(flops=flops, bytes_accessed=size, transcendentals=0),
        compiler_params=pltpu.CompilerParams(vmem_limit_bytes=limit << 10),
    )(*ins)


def tri_rows(get):
    return jnp.concatenate([get(p, 8) for p in range(8)] + [get(p, 16) for p in range(8, 16)], axis=0)


def pieces(x):
    hi = x.astype(jnp.bfloat16).astype(F32)
    rest = x - hi
    mid = rest.astype(jnp.bfloat16).astype(F32)
    low = (rest - mid).astype(jnp.bfloat16).astype(F32)
    return hi, mid, low


def first_kernel(n_lat, reach_ref, fac_hbm, land_hbm, cell_hbm, value_hbm, weight_hbm, inverse_hbm, south_ref, north_ref, diag_ref,
                 rhs_ref, ocean_ref, send_ref, extra_ref, first, last, wide, cell_ref, value_ref, weight_ref, left, right,
                 inverse_ref, sems):
    moves = (
        (cell_hbm, cell_ref),
        (value_hbm, value_ref),
        (weight_hbm, weight_ref),
        (land_hbm, wide.at[pl.ds(HW, COLS), :]),
        (fac_hbm.at[0], first),
        (fac_hbm.at[BLK + 1], last),
        (inverse_hbm, inverse_ref),
    )
    copies = [pltpu.make_async_copy(src, dst, sems.at[n]) for n, (src, dst) in enumerate(moves)]
    for copy in copies:
        copy.start()
    me = lax.axis_index("lat")
    wide[0:HW, :] = jnp.zeros((HW, ROWS), jnp.int32)
    wide[HW + COLS : EXT, :] = jnp.zeros((HW, ROWS), jnp.int32)
    for copy in copies[:4]:
        copy.wait()
    ocean = jnp.transpose(wide[...].astype(F32))
    ocean_ref[...] = ocean
    step = 512
    for start in range(0, OBS, step):
        cut = slice(start, start + step)
        cell = cell_ref[:, cut]
        at_row = ((cell >> 5) * 9363) >> 16
        at_col = cell - at_row * COLS + HW
        weight = weight_ref[:, cut]
        parts = pieces(weight) + pieces(weight * value_ref[:, cut])
        hit = iota((ROWS, step), 0) == at_row
        for n, part in enumerate(parts):
            left[n * ROWS : (n + 1) * ROWS, cut] = jnp.where(hit, part, 0.0).astype(jnp.bfloat16)
        right[:, cut] = jnp.where(iota((EXT, step), 0) == at_col, 1.0, 0.0).astype(jnp.bfloat16)
    sums = lax.dot_general(left[...], right[...], (((1,), (1,)), ((), ())), preferred_element_type=F32)
    part = [sums[n * ROWS : (n + 1) * ROWS] for n in range(6)]
    diag_ref[...] = part[0] + (part[1] + part[2])
    rhs = ocean * (part[3] + (part[4] + part[5]))
    rhs_ref[...] = rhs
    sub = iota((16, EXT), 0)
    lane = iota((16, EXT), 1)
    pooled = jnp.zeros((16, EXT), F32)
    for s in range(4):
        band = jnp.sum(rhs[s * 32 : s * 32 + 32], axis=0, keepdims=True)
        pooled = jnp.where((sub >> 2) == s, band, pooled)
    begin = HW + (sub & 3) * 56
    pooled = jnp.where((lane >= begin) & (lane < begin + 56), pooled, 0.0)
    coarse = jnp.sum(pooled, axis=1, keepdims=True)
    n_row = n_lat * 16 // 128
    placed = jnp.sum(jnp.where(lane == sub + 16 * me, coarse, 0.0), axis=0, keepdims=True)
    for p in range(n_lat):
        for r in range(n_row):
            send_ref[p, r : r + 1, :] = placed[:, r * 128 : (r + 1) * 128]
        face = jnp.where(p < me, ocean[0:1], ocean[ROWS - 1 : ROWS])
        send_ref[p, n_row : n_row + 1, :] = face[:, 0:128]
        send_ref[p, n_row + 1 : n_row + 2, :] = face[:, 128:256]
    for copy in copies[4:6]:
        copy.wait()
    edge = iota((TRI, EXT), 1)
    row = iota((TRI, EXT), 0)
    q = jnp.where(row < 64, row & 7, row & 15)
    reach = reach_ref[0, 0]
    inside = (edge >= HW - reach) & (edge < HW + COLS + reach)
    north_ref[...] = jnp.where(inside & (q >= HW - reach), tri_rows(lambda p, n: first[p, 0:n, :]), 0.0)
    south_ref[...] = jnp.where(inside & (q < reach), tri_rows(lambda p, n: last[p, 0:n, :]), 0.0)
    side_lane = iota((16, EXT), 1)
    for half, face, edge in ((0, 16, 0), (1, 239, 15)):
        load = jnp.zeros((16, EXT), F32)
        mask = jnp.zeros((16, EXT), F32)
        for k in range(BLK):
            spots = (side_lane == k * 16 + edge) | (side_lane == 160 + k)
            if k == 0:
                spots = spots | (side_lane == 128 + edge) | (side_lane == 168)
            if k == BLK - 1:
                spots = spots | (side_lane == 144 + edge) | (side_lane == 169)
            load = jnp.where(spots, rhs[k * 16 : k * 16 + 16, face : face + 1], load)
            mask = jnp.where(spots, ocean[k * 16 : k * 16 + 16, face : face + 1], mask)
        extra_ref[half, 0:16, :] = load
        extra_ref[half, 16:32, :] = mask
    copies[6].wait()
    for half in range(2):
        for m in range(inverse_ref.shape[1] // EXT):
            for t in range(4):
                at_row, source = 32 + 4 * m + t, 4 * t + 3 * half
                extra_ref[half, at_row : at_row + 1, :] = inverse_ref[source : source + 1, m * EXT : (m + 1) * EXT]


def side_kernel(n_lon, n_row, reach_ref, fac_ref, from_n_ref, from_s_ref, extra_ref, got_ref, to_e_ref,
                to_w_ref, send_ref):
    reach = reach_ref[0, 0]
    lane = iota((TRI, 128), 1)
    for ref, half, face, start in ((to_e_ref, 1, 111, 112), (to_w_ref, 0, 16, 0)):
        lanes = slice(half * 128, half * 128 + 128)
        bulk = jnp.zeros((TRI, 128), F32)
        rest = jnp.zeros((TRI, 128), F32)
        for k in range(BLK):
            block = tri_rows(lambda p, n: fac_ref[k + 1, p, 0:n, lanes])
            at = lane - k * 16
            own = (at >= 0) & (at < jnp.minimum(reach, 16)) if half else (at >= HW - reach) & (at < 16)
            shift = (k * 16 - start) % 128
            bulk = jnp.where(own, pltpu.roll(block, shift, 1) if shift else block, bulk)
            rest = jnp.where(lane == 32 + k, pltpu.roll(block, (32 + k - face) % 128, 1), rest)
        north, south = from_n_ref[:, lanes], from_s_ref[:, lanes]
        rest = jnp.where(lane < 16, pltpu.roll(north, 16, 1) if half else north, rest)
        rest = jnp.where((lane >= 16) & (lane < 32), pltpu.roll(south, 32 if half else 16, 1), rest)
        rest = jnp.where(lane == 40, pltpu.roll(north, (40 - face) % 128, 1), rest)
        rest = jnp.where(lane == 41, pltpu.roll(south, (41 - face) % 128, 1), rest)
        ref[0:TRI, 0:128] = bulk
        ref[0:TRI, 128:256] = rest
        ref[TRI:, :] = extra_ref[half]
    total = jnp.sum(got_ref[:, 0:n_row, :], axis=0)
    for p in range(n_lon):
        send_ref[p] = total


def apply_block(u, get):
    low = u[0:8]
    g_low = jnp.zeros_like(low)
    g_high = jnp.zeros_like(low)
    for p in range(8):
        line = get(p, 8)
        f = jnp.sum(line * low, axis=0, keepdims=True)
        g_low = g_low + line * f
    for p in range(8, 16):
        line = get(p, 16)
        f = jnp.sum(line * u, axis=0, keepdims=True)
        g = line * f
        g_low = g_low + g[0:8]
        g_high = g_high + g[8:16]
    return jnp.concatenate([g_low, g_high], axis=0)


def tri_get(ref):
    def get(p, n):
        start = p * 8 if p < 8 else 64 + (p - 8) * 16
        return ref[start : start + n, :]

    return get


def solve_kernel(n_lat, n_lon, n_row, fac_ref, rhs_ref, ocean_ref, diag_ref, to_w_ref, to_e_ref, from_w_ref, from_e_ref,
                 from_n_ref, from_s_ref, inverse_ref, got_ref, coarse_ref, z_ref, image_ref, send_ref, acc, z_pad, o_pad):
    me = lax.axis_index("lat")
    lane = iota((16, 128), 1)
    wide_lane = iota((16, EXT), 1)
    u_w = jnp.zeros((16, 128), F32)
    u_e = jnp.zeros((16, 128), F32)
    for k in range(BLK):
        rows = slice(k * 16, k * 16 + 16)
        u = rhs_ref[rows, :]
        acc[rows, :] = apply_block(u, lambda p, n: fac_ref[k + 1, p, 0:n, :])
        own = (lane >= k * 16) & (lane < k * 16 + 16)
        u_w = jnp.where(own, pltpu.roll(u[:, 0:128], (k * 16 - 16) % 128, 1), u_w)
        u_e = jnp.where(own, pltpu.roll(u[:, 128:256], (k * 16 - 96) % 128, 1), u_e)
    top, end = rhs_ref[0:16, :], rhs_ref[ROWS - 16 : ROWS, :]

    def corners(top, end, at):
        return jnp.where(
            lane < 16, pltpu.roll(top, (-at) % 128, 1), jnp.where(lane < 32, pltpu.roll(end, (16 - at) % 128, 1), 0.0)
        )

    ring_w, ring_e = from_w_ref[TRI : TRI + 16, :], from_e_ref[TRI : TRI + 16, :]
    u_w = jnp.concatenate([u_w, corners(top[:, 0:128], end[:, 0:128], 16)], axis=1)
    u_e = jnp.concatenate([u_e, corners(top[:, 128:256], end[:, 128:256], 96)], axis=1)
    u_w = jnp.where(wide_lane >= 160, ring_w, u_w)
    u_e = jnp.where(wide_lane >= 160, ring_e, u_e)
    g_w = apply_block(u_w, tri_get(from_w_ref))
    g_e = apply_block(u_e, tri_get(from_e_ref))
    h_w = apply_block(ring_w, tri_get(to_w_ref))
    h_e = apply_block(ring_e, tri_get(to_e_ref))
    in_w = (lane >= 16) & (lane < 32)
    in_e = (lane >= 96) & (lane < 112)
    for k in range(BLK):
        rows = slice(k * 16, k * 16 + 16)
        add_w = pltpu.roll(g_w[:, 0:128], (16 - k * 16) % 128, 1)
        add_e = pltpu.roll(g_e[:, 0:128], (96 - k * 16) % 128, 1)
        if k == 0:
            add_w = add_w + pltpu.roll(g_w[:, 128:256], 16, 1)
            add_e = add_e + pltpu.roll(g_e[:, 128:256], 96, 1)
        if k == BLK - 1:
            add_w = add_w + g_w[:, 128:256]
            add_e = add_e + pltpu.roll(g_e[:, 128:256], 80, 1)
        acc[rows, 0:128] += jnp.where(in_w, add_w, 0.0)
        acc[rows, 128:256] += jnp.where(in_e, add_e, 0.0)
    for rows, ref in ((slice(0, 16), from_n_ref), (slice(ROWS - 16, ROWS), from_s_ref)):
        acc[rows, :] += apply_block(rhs_ref[rows, :], tri_get(ref))
    dot = jnp.zeros((16, EXT), F32)
    dot_w = jnp.zeros((4, EXT), F32)
    dot_e = jnp.zeros((4, EXT), F32)
    for m in range(n_lon * n_row // 2):
        part = [coarse_ref[n // n_row, n % n_row : n % n_row + 1, :] for n in (2 * m, 2 * m + 1)]
        part = jnp.concatenate(part, axis=1)
        dot = dot + inverse_ref[:, m * EXT : (m + 1) * EXT] * part
        at_row = TRI + 32 + 4 * m
        dot_w = dot_w + from_w_ref[at_row : at_row + 4, :] * part
        dot_e = dot_e + from_e_ref[at_row : at_row + 4, :] * part
    answer = jnp.sum(dot, axis=1, keepdims=True)
    answer_w = jnp.sum(dot_w, axis=1, keepdims=True)
    answer_e = jnp.sum(dot_e, axis=1, keepdims=True)
    sub = iota((16, EXT), 0)
    first = HW + (sub & 3) * 56
    spread = jnp.where((wide_lane >= first) & (wide_lane < first + 56), answer, 0.0)
    for k in range(BLK):
        rows = slice(k * 16, k * 16 + 16)
        s = k // 2
        band = jnp.sum(jnp.where((sub >> 2) == s, spread, 0.0), axis=0, keepdims=True)
        ocean = ocean_ref[rows, :]
        z = ocean * (acc[rows, :] + band)
        z_ref[rows, :] = z

        def edge(g, h, ref, at, answer):
            ring = h[:, k * 16 + at : k * 16 + at + 1] + g[:, 160 + k : 161 + k]
            if k == 0:
                ring = ring + (h[:, 128 + at : 129 + at] + g[:, 168:169])
            if k == BLK - 1:
                ring = ring + (h[:, 144 + at : 145 + at] + g[:, 169:170])
            mask = ref[TRI + 16 : TRI + 32, 160 + k : 161 + k]
            return mask, mask * (ring + answer[s : s + 1])

        o_w, z_w = edge(g_w, h_w, from_w_ref, 15, answer_w)
        o_e, z_e = edge(g_e, h_e, from_e_ref, 0, answer_e)
        z_pad[rows, :] = jnp.where(wide_lane == 15, z_w, jnp.where(wide_lane == 240, z_e, z))
        o_pad[rows, :] = jnp.where(wide_lane == 15, o_w, jnp.where(wide_lane == 240, o_e, ocean))

    row = iota((ROWS, EXT), 0)
    z = z_ref[...]
    ocean = ocean_ref[...]

    def sides(x):
        return pltpu.roll(x, 1, 1) + pltpu.roll(x, EXT - 1, 1)

    def line(index, inside):
        face = jnp.concatenate([got_ref[index, n_row : n_row + 1, :], got_ref[index, n_row + 1 : n_row + 2, :]], axis=1)
        return jnp.where(inside, face, 0.0)

    o_north = line(jnp.maximum(me - 1, 0), me > 0)
    o_south = line(jnp.minimum(me + 1, n_lat - 1), me < n_lat - 1)

    def rows(x, north, south):
        return jnp.where(row == 0, north, pltpu.roll(x, 1, 0)) + jnp.where(
            row == ROWS - 1, south, pltpu.roll(x, ROWS - 1, 0)
        )

    total = sides(o_pad[...]) + rows(ocean, o_north, o_south)
    beside = sides(z_pad[...]) + rows(z, 0.0, 0.0)
    image = ocean * ((diag_ref[...] + DAMPING) * z + (total * z - beside)) + (1.0 - ocean) * z
    image_ref[...] = image
    affinity = jnp.sum(jnp.sum(rhs_ref[...] * z, axis=0, keepdims=True), axis=1, keepdims=True)
    energy = jnp.sum(jnp.sum(z * image, axis=0, keepdims=True), axis=1, keepdims=True)
    small = iota((1, 128), 1)
    scalars = jnp.where(small == 0, affinity, jnp.where(small == 1, energy, 0.0))
    for p in range(n_lat):
        send_ref[p, 0:1, :] = z[0:1, 0:128]
        send_ref[p, 1:2, :] = z[0:1, 128:256]
        send_ref[p, 2:3, :] = z[ROWS - 1 : ROWS, 0:128]
        send_ref[p, 3:4, :] = z[ROWS - 1 : ROWS, 128:256]
        send_ref[p, 4:5, :] = scalars


def cross_kernel(n_lat, n_lon, got_ref, send_ref):
    cross = jnp.zeros((2, 128), F32)
    for i in range(n_lat - 1):
        cross = cross + got_ref[i, 2:4, :] * got_ref[i + 1, 0:2, :]
    cross = jnp.sum(jnp.sum(cross, axis=0, keepdims=True), axis=1, keepdims=True)
    small = iota((1, 128), 1)
    total = jnp.sum(got_ref[:, 4:5, :], axis=0) - jnp.where(small == 1, 2.0 * cross, 0.0)
    for p in range(n_lon):
        send_ref[p] = total


def final_kernel(n_lat, z_ref, image_ref, rhs_ref, ocean_ref, got_ref, sums_ref, sol_ref, res_ref, pre_ref):
    me = lax.axis_index("lat")
    row = iota((ROWS, EXT), 0)
    z = z_ref[...]
    sums = jnp.sum(sums_ref[...], axis=0)
    small = iota((1, 128), 1)
    affinity = jnp.sum(jnp.where(small == 0, sums, 0.0), axis=1, keepdims=True)
    energy = jnp.sum(jnp.where(small == 1, sums, 0.0), axis=1, keepdims=True)
    alpha = affinity / energy

    def line(index, first, inside):
        face = jnp.concatenate([got_ref[index, first : first + 1, :], got_ref[index, first + 1 : first + 2, :]], axis=1)
        return jnp.where(inside, face, 0.0)

    z_north = line(jnp.maximum(me - 1, 0), 2, me > 0)
    z_south = line(jnp.minimum(me + 1, n_lat - 1), 0, me < n_lat - 1)
    edge = jnp.where(row == 0, z_north, jnp.where(row == ROWS - 1, z_south, 0.0))
    image = image_ref[...] - ocean_ref[...] * edge

    def store(ref, x):
        ref[...] = jnp.transpose(x)[HW : HW + COLS, :]

    store(pre_ref, z)
    store(sol_ref, alpha * z)
    store(res_ref, rhs_ref[...] - alpha * image)


def body(land_sea, obs_cell, obs_value, obs_weight, intersection, factors, coarse_inverse):
    n_lat, n_lon = lax.axis_size("lat"), lax.axis_size("lon")
    n_row = n_lat * 16 // 128
    ring = [(j, (j + 1) % n_lon) for j in range(n_lon)]
    back = [(b, a) for a, b in ring]
    line = [(i, i + 1) for i in range(n_lat - 1)]
    up = [(b, a) for a, b in line]
    tile = (ROWS, EXT)

    def k(kernel, *static):
        def run(*refs):
            kernel(*static, *refs)

        run.__name__ = kernel.__name__
        return run

    slab = (TRI, EXT)
    more = 32 + 4 * coarse_inverse.shape[1] // EXT
    to_s, to_n, diag, rhs, ocean, send, extra = call(
        k(first_kernel, n_lat),
        [slab, slab, tile, tile, tile, (n_lat, n_row + 2, 128), (2, more, EXT)],
        (
            intersection,
            *(
                pltpu.with_memory_space_constraint(x, pltpu.HBM)
                for x in (
                    factors,
                    land_sea.T,
                    obs_cell.reshape(1, OBS),
                    obs_value.reshape(1, OBS),
                    obs_weight.reshape(1, OBS),
                    coarse_inverse,
                )
            ),
        ),
        places="shhhhhh",
        limit=16384,
        scratch=[
            pltpu.VMEM((16, 16, EXT), F32),
            pltpu.VMEM((16, 16, EXT), F32),
            pltpu.VMEM((EXT, ROWS), jnp.int32),
            pltpu.VMEM((1, OBS), jnp.int32),
            pltpu.VMEM((1, OBS), F32),
            pltpu.VMEM((1, OBS), F32),
            pltpu.VMEM((6 * ROWS, OBS), jnp.bfloat16),
            pltpu.VMEM((EXT, OBS), jnp.bfloat16),
            pltpu.VMEM(coarse_inverse.shape, F32),
            pltpu.SemaphoreType.DMA((7,)),
        ],
    )
    from_n = lax.ppermute(to_s, "lat", line)
    from_s = lax.ppermute(to_n, "lat", up)
    got = lax.all_to_all(send, "lat", 0, 0, tiled=True)
    message = (TRI + more, EXT)
    to_e, to_w, send = call(
        k(side_kernel, n_lon, n_row),
        [message, message, (n_lon, n_row, 128)],
        (intersection, factors, from_n, from_s, extra, got),
        places="svvvvv",
    )
    from_w = lax.ppermute(to_e, "lon", ring)
    from_e = lax.ppermute(to_w, "lon", back)
    coarse = lax.all_to_all(send, "lon", 0, 0, tiled=True)
    z, image, send = call(
        k(solve_kernel, n_lat, n_lon, n_row),
        [tile, tile, (n_lat, 5, 128)],
        (factors, rhs, ocean, diag, to_w, to_e, from_w, from_e, from_n, from_s, coarse_inverse, got, coarse),
        scratch=[pltpu.VMEM(tile, F32), pltpu.VMEM(tile, F32), pltpu.VMEM(tile, F32)],
    )
    edges = lax.all_to_all(send, "lat", 0, 0, tiled=True)
    (send,) = call(k(cross_kernel, n_lat, n_lon), [(n_lon, 1, 128)], (edges,))
    sums = lax.all_to_all(send, "lon", 0, 0, tiled=True)
    out = (COLS, ROWS)
    return tuple(
        x.T for x in call(k(final_kernel, n_lat), [out, out, out], (z, image, rhs, ocean, edges, sums))
    )


def solution(mesh):
    in_specs = (
        P("lat", "lon"),
        P("lat", "lon", None),
        P("lat", "lon", None),
        P("lat", "lon", None),
        P("lat", "lon"),
        P("lat", None, None, "lon"),
        P(("lon", "lat"), None),
    )
    out_specs = (P("lat", "lon"), P("lat", "lon"), P("lat", "lon"))
    return jax.shard_map(body, mesh=mesh, in_specs=in_specs, out_specs=out_specs, check_vma=False)
```

```python
import jax
import jax.numpy as jnp
from jax import lax
from jax.experimental import pallas as pl
from jax.experimental.pallas import tpu as pltpu
from jax.sharding import PartitionSpec as P

F32 = jnp.float32
DAMPING = 0.02
ROWS, COLS, HW, EXT = 128, 224, 16, 256
BLK = 8
TRI = 192
OBS = 2048
RING = ([170] + [144 + 16 * k for k in range(1, 7)] + [171], [255, 170, 171] + [127 + 16 * k for k in range(3, 8)])

VM = pl.BlockSpec(memory_space=pltpu.VMEM)
PLACES = {
    "v": VM,
    "s": pl.BlockSpec(memory_space=pltpu.SMEM),
    "h": pl.BlockSpec(memory_space=pltpu.HBM),
}


def iota(shape, dim):
    return lax.broadcasted_iota(jnp.int32, shape, dim)


def call(kernel, outs, ins, scratch=(), flops=100000, limit=16384, places=None):
    size = sum(4 * x.size for x in ins)
    return pl.pallas_call(
        kernel,
        out_shape=[jax.ShapeDtypeStruct(s, F32) for s in outs],
        in_specs=[PLACES[p] for p in places or "v" * len(ins)],
        out_specs=[VM] * len(outs),
        scratch_shapes=list(scratch),
        cost_estimate=pl.CostEstimate(flops=flops, bytes_accessed=size, transcendentals=0),
        compiler_params=pltpu.CompilerParams(vmem_limit_bytes=limit << 10),
    )(*ins)


def tri_rows(get):
    return jnp.concatenate([get(p, 8) for p in range(8)] + [get(p, 16) for p in range(8, 16)], axis=0)


def pieces(x):
    hi = x.astype(jnp.bfloat16).astype(F32)
    rest = x - hi
    mid = rest.astype(jnp.bfloat16).astype(F32)
    low = (rest - mid).astype(jnp.bfloat16).astype(F32)
    return hi, mid, low


def first_kernel(n_lat, reach_ref, fac_hbm, land_hbm, cell_hbm, value_hbm, weight_hbm, inverse_hbm, south_ref, north_ref, diag_ref,
                 rhs_ref, ocean_ref, send_ref, extra_ref, first, last, wide, cell_ref, value_ref, weight_ref, left, right,
                 inverse_ref, sems):
    moves = (
        (cell_hbm, cell_ref),
        (value_hbm, value_ref),
        (weight_hbm, weight_ref),
        (land_hbm, wide.at[pl.ds(HW, COLS), :]),
        (fac_hbm.at[0], first),
        (fac_hbm.at[BLK + 1], last),
        (inverse_hbm, inverse_ref),
    )
    copies = [pltpu.make_async_copy(src, dst, sems.at[n]) for n, (src, dst) in enumerate(moves)]
    for copy in copies:
        copy.start()
    me = lax.axis_index("lat")
    wide[0:HW, :] = jnp.zeros((HW, ROWS), jnp.int32)
    wide[HW + COLS : EXT, :] = jnp.zeros((HW, ROWS), jnp.int32)
    for copy in copies[:4]:
        copy.wait()
    ocean = jnp.transpose(wide[...].astype(F32))
    ocean_ref[...] = ocean
    step = 512
    for start in range(0, OBS, step):
        cut = slice(start, start + step)
        cell = cell_ref[:, cut]
        at_row = ((cell >> 5) * 9363) >> 16
        at_col = cell - at_row * COLS + HW
        weight = weight_ref[:, cut]
        parts = pieces(weight) + pieces(weight * value_ref[:, cut])
        hit = iota((ROWS, step), 0) == at_row
        for n, part in enumerate(parts):
            left[n * ROWS : (n + 1) * ROWS, cut] = jnp.where(hit, part, 0.0).astype(jnp.bfloat16)
        right[:, cut] = jnp.where(iota((EXT, step), 0) == at_col, 1.0, 0.0).astype(jnp.bfloat16)
    sums = lax.dot_general(left[...], right[...], (((1,), (1,)), ((), ())), preferred_element_type=F32)
    part = [sums[n * ROWS : (n + 1) * ROWS] for n in range(6)]
    diag_ref[...] = part[0] + (part[1] + part[2])
    rhs = ocean * (part[3] + (part[4] + part[5]))
    rhs_ref[...] = rhs
    sub = iota((16, EXT), 0)
    lane = iota((16, EXT), 1)
    pooled = jnp.zeros((16, EXT), F32)
    for s in range(4):
        band = jnp.sum(rhs[s * 32 : s * 32 + 32], axis=0, keepdims=True)
        pooled = jnp.where((sub >> 2) == s, band, pooled)
    begin = HW + (sub & 3) * 56
    pooled = jnp.where((lane >= begin) & (lane < begin + 56), pooled, 0.0)
    coarse = jnp.sum(pooled, axis=1, keepdims=True)
    spare = jnp.sum(jnp.where(lane == sub, coarse, 0.0), axis=0, keepdims=True)
    edge_lane = iota((1, EXT), 1)
    for p in range(n_lat):
        face = jnp.where(edge_lane < HW, spare, jnp.where(p < me, ocean[0:1], ocean[ROWS - 1 : ROWS]))
        send_ref[p, 0:1, :] = face[:, 0:128]
        send_ref[p, 1:2, :] = face[:, 128:256]
    for copy in copies[4:6]:
        copy.wait()
    edge = iota((TRI, EXT), 1)
    row = iota((TRI, EXT), 0)
    q = jnp.where(row < 64, row & 7, row & 15)
    reach = reach_ref[0, 0]
    inside = (edge >= HW - reach) & (edge < HW + COLS + reach)
    north_ref[...] = jnp.where(inside & (q >= HW - reach), tri_rows(lambda p, n: first[p, 0:n, :]), 0.0)
    south_ref[...] = jnp.where(inside & (q < reach), tri_rows(lambda p, n: last[p, 0:n, :]), 0.0)
    side_lane = iota((16, EXT), 1)
    for half, face, edge in ((0, 16, 0), (1, 239, 15)):
        load = jnp.zeros((16, EXT), F32)
        mask = jnp.zeros((16, EXT), F32)
        for k in range(BLK):
            spots = (side_lane == k * 16 + edge) | (side_lane == RING[half][k])
            if k == 0:
                spots = spots | (side_lane == 128 + edge) | (side_lane == 168)
            if k == BLK - 1:
                spots = spots | (side_lane == 144 + edge) | (side_lane == 169)
            load = jnp.where(spots, rhs[k * 16 : k * 16 + 16, face : face + 1], load)
            mask = jnp.where(spots, ocean[k * 16 : k * 16 + 16, face : face + 1], mask)
        extra_ref[half, 0:16, :] = load
        extra_ref[half, 16:32, :] = mask
    copies[6].wait()
    for half in range(2):
        for m in range(inverse_ref.shape[1] // EXT):
            for t in range(4):
                at_row, source = 32 + 4 * m + t, 4 * t + 3 * half
                extra_ref[half, at_row : at_row + 1, :] = inverse_ref[source : source + 1, m * EXT : (m + 1) * EXT]


def side_kernel(n_lon, n_row, reach_ref, fac_ref, from_n_ref, from_s_ref, extra_ref, got_ref, to_e_ref,
                to_w_ref, send_ref):
    reach = reach_ref[0, 0]
    lane = iota((TRI, 128), 1)
    for ref, half, face, start in ((to_e_ref, 1, 111, 112), (to_w_ref, 0, 16, 0)):
        lanes = slice(half * 128, half * 128 + 128)
        bulk = jnp.zeros((TRI, 128), F32)
        rest = jnp.zeros((TRI, 128), F32)
        for k in range(BLK):
            block = tri_rows(lambda p, n: fac_ref[k + 1, p, 0:n, lanes])
            at = lane - k * 16
            own = (at >= 0) & (at < jnp.minimum(reach, 16)) if half else (at >= HW - reach) & (at < 16)
            shift = (k * 16 - start) % 128
            moved = pltpu.roll(block, shift, 1) if shift else block
            bulk = jnp.where(own, moved, bulk)
            ring = RING[half][k] - 128
            if (face + shift) % 128 != ring:
                moved = pltpu.roll(block, (ring - face) % 128, 1)
            rest = jnp.where(lane == ring, moved, rest)
        north, south = from_n_ref[:, lanes], from_s_ref[:, lanes]
        rest = jnp.where(lane < 16, pltpu.roll(north, 16, 1) if half else north, rest)
        rest = jnp.where((lane >= 16) & (lane < 32), pltpu.roll(south, 32 if half else 16, 1), rest)
        rest = jnp.where(lane == 40, pltpu.roll(north, (40 - face) % 128, 1), rest)
        rest = jnp.where(lane == 41, pltpu.roll(south, (41 - face) % 128, 1), rest)
        ref[0:TRI, 0:128] = bulk
        ref[0:TRI, 128:256] = rest
        ref[TRI:, :] = extra_ref[half]
    small = iota((1, 128), 1)
    total = [jnp.zeros((1, 128), F32) for _ in range(n_row)]
    for p in range(n_row * 8):
        at = p * 16 % 128
        part = pltpu.roll(got_ref[p, 0:1, :], at, 1) if at else got_ref[p, 0:1, :]
        total[p // 8] = jnp.where((small >= at) & (small < at + 16), part, total[p // 8])
    for p in range(n_lon):
        for r in range(n_row):
            send_ref[p, r : r + 1, :] = total[r]


def apply_block(u, get):
    low = u[0:8]
    g_low = jnp.zeros_like(low)
    g_high = jnp.zeros_like(low)
    for p in range(8):
        line = get(p, 8)
        f = jnp.sum(line * low, axis=0, keepdims=True)
        g_low = g_low + line * f
    for p in range(8, 16):
        line = get(p, 16)
        f = jnp.sum(line * u, axis=0, keepdims=True)
        g = line * f
        g_low = g_low + g[0:8]
        g_high = g_high + g[8:16]
    return jnp.concatenate([g_low, g_high], axis=0)


def tri_get(ref):
    def get(p, n):
        start = p * 8 if p < 8 else 64 + (p - 8) * 16
        return ref[start : start + n, :]

    return get


def solve_kernel(n_lat, n_lon, n_row, fac_ref, rhs_ref, ocean_ref, diag_ref, to_w_ref, to_e_ref, from_w_ref, from_e_ref,
                 from_n_ref, from_s_ref, inverse_ref, got_ref, coarse_ref, z_ref, image_ref, send_ref, acc, z_pad, o_pad):
    me = lax.axis_index("lat")
    lane = iota((16, 128), 1)
    wide_lane = iota((16, EXT), 1)
    u_w = jnp.zeros((16, 128), F32)
    u_e = jnp.zeros((16, 128), F32)
    for k in range(BLK):
        rows = slice(k * 16, k * 16 + 16)
        u = rhs_ref[rows, :]
        acc[rows, :] = apply_block(u, lambda p, n: fac_ref[k + 1, p, 0:n, :])
        own = (lane >= k * 16) & (lane < k * 16 + 16)
        u_w = jnp.where(own, pltpu.roll(u[:, 0:128], (k * 16 - 16) % 128, 1), u_w)
        u_e = jnp.where(own, pltpu.roll(u[:, 128:256], (k * 16 - 96) % 128, 1), u_e)
    top, end = rhs_ref[0:16, :], rhs_ref[ROWS - 16 : ROWS, :]

    def corners(top, end, at):
        return jnp.where(
            lane < 16, pltpu.roll(top, (-at) % 128, 1), jnp.where(lane < 32, pltpu.roll(end, (16 - at) % 128, 1), 0.0)
        )

    ring_w, ring_e = from_w_ref[TRI : TRI + 16, :], from_e_ref[TRI : TRI + 16, :]
    u_w = jnp.concatenate([u_w, corners(top[:, 0:128], end[:, 0:128], 16)], axis=1)
    u_e = jnp.concatenate([u_e, corners(top[:, 128:256], end[:, 128:256], 96)], axis=1)
    u_w = jnp.where(wide_lane >= 160, ring_w, u_w)
    u_e = jnp.where(wide_lane >= 160, ring_e, u_e)
    g_w = apply_block(u_w, tri_get(from_w_ref))
    g_e = apply_block(u_e, tri_get(from_e_ref))
    own_w, own_e = tri_get(to_w_ref), tri_get(to_e_ref)

    def own_get(p, n):
        return jnp.where((wide_lane[0:n] & 15) == 0, own_e(p, n), own_w(p, n))

    h = apply_block(jnp.where((wide_lane & 15) == 0, ring_e, ring_w), own_get)
    in_w = (lane >= 16) & (lane < 32)
    in_e = (lane >= 96) & (lane < 112)
    for k in range(BLK):
        rows = slice(k * 16, k * 16 + 16)
        add_w = pltpu.roll(g_w[:, 0:128], (16 - k * 16) % 128, 1)
        add_e = pltpu.roll(g_e[:, 0:128], (96 - k * 16) % 128, 1)
        if k == 0:
            add_w = add_w + pltpu.roll(g_w[:, 128:256], 16, 1)
            add_e = add_e + pltpu.roll(g_e[:, 128:256], 96, 1)
        if k == BLK - 1:
            add_w = add_w + g_w[:, 128:256]
            add_e = add_e + pltpu.roll(g_e[:, 128:256], 80, 1)
        acc[rows, 0:128] += jnp.where(in_w, add_w, 0.0)
        acc[rows, 128:256] += jnp.where(in_e, add_e, 0.0)
    for rows, ref in ((slice(0, 16), from_n_ref), (slice(ROWS - 16, ROWS), from_s_ref)):
        acc[rows, :] += apply_block(rhs_ref[rows, :], tri_get(ref))
    dot = jnp.zeros((16, EXT), F32)
    dot_w = jnp.zeros((4, EXT), F32)
    dot_e = jnp.zeros((4, EXT), F32)
    for m in range(n_lon * n_row // 2):
        part = [coarse_ref[n // n_row, n % n_row : n % n_row + 1, :] for n in (2 * m, 2 * m + 1)]
        part = jnp.concatenate(part, axis=1)
        dot = dot + inverse_ref[:, m * EXT : (m + 1) * EXT] * part
        at_row = TRI + 32 + 4 * m
        dot_w = dot_w + from_w_ref[at_row : at_row + 4, :] * part
        dot_e = dot_e + from_e_ref[at_row : at_row + 4, :] * part
    answer = jnp.sum(dot, axis=1, keepdims=True)
    answer_w = jnp.sum(dot_w, axis=1, keepdims=True)
    answer_e = jnp.sum(dot_e, axis=1, keepdims=True)
    sub = iota((16, EXT), 0)
    first = HW + (sub & 3) * 56
    spread = jnp.where((wide_lane >= first) & (wide_lane < first + 56), answer, 0.0)
    for k in range(BLK):
        rows = slice(k * 16, k * 16 + 16)
        s = k // 2
        band = jnp.sum(jnp.where((sub >> 2) == s, spread, 0.0), axis=0, keepdims=True)
        ocean = ocean_ref[rows, :]
        z = ocean * (acc[rows, :] + band)
        z_ref[rows, :] = z

        def edge(g, ref, at, spot, answer):
            ring = h[:, k * 16 + at : k * 16 + at + 1] + g[:, spot : spot + 1]
            if k == 0:
                ring = ring + (h[:, 128 + at : 129 + at] + g[:, 168:169])
            if k == BLK - 1:
                ring = ring + (h[:, 144 + at : 145 + at] + g[:, 169:170])
            mask = ref[TRI + 16 : TRI + 32, spot : spot + 1]
            return mask, mask * (ring + answer[s : s + 1])

        o_w, z_w = edge(g_w, from_w_ref, 15, RING[1][k], answer_w)
        o_e, z_e = edge(g_e, from_e_ref, 0, RING[0][k], answer_e)
        z_pad[rows, :] = jnp.where(wide_lane == 15, z_w, jnp.where(wide_lane == 240, z_e, z))
        o_pad[rows, :] = jnp.where(wide_lane == 15, o_w, jnp.where(wide_lane == 240, o_e, ocean))

    row = iota((ROWS, EXT), 0)
    z = z_ref[...]
    ocean = ocean_ref[...]

    def sides(x):
        return pltpu.roll(x, 1, 1) + pltpu.roll(x, EXT - 1, 1)

    def line(index, inside):
        face = jnp.concatenate([got_ref[index, 0:1, :], got_ref[index, 1:2, :]], axis=1)
        return jnp.where(inside & (iota((1, EXT), 1) >= HW), face, 0.0)

    o_north = line(jnp.maximum(me - 1, 0), me > 0)
    o_south = line(jnp.minimum(me + 1, n_lat - 1), me < n_lat - 1)

    def rows(x, north, south):
        return jnp.where(row == 0, north, pltpu.roll(x, 1, 0)) + jnp.where(
            row == ROWS - 1, south, pltpu.roll(x, ROWS - 1, 0)
        )

    total = sides(o_pad[...]) + rows(ocean, o_north, o_south)
    beside = sides(z_pad[...]) + rows(z, 0.0, 0.0)
    image = ocean * ((diag_ref[...] + DAMPING) * z + (total * z - beside)) + (1.0 - ocean) * z
    image_ref[...] = image
    affinity = jnp.sum(jnp.sum(rhs_ref[...] * z, axis=0, keepdims=True), axis=1, keepdims=True)
    energy = jnp.sum(jnp.sum(z * image, axis=0, keepdims=True), axis=1, keepdims=True)
    small = iota((1, 128), 1)
    scalars = jnp.where(small == 0, affinity, jnp.where(small == 1, energy, 0.0))
    for p in range(n_lat):
        send_ref[p, 0:1, :] = jnp.where(small < 2, scalars, z[0:1, 0:128])
        send_ref[p, 1:2, :] = z[0:1, 128:256]
        send_ref[p, 2:3, :] = z[ROWS - 1 : ROWS, 0:128]
        send_ref[p, 3:4, :] = z[ROWS - 1 : ROWS, 128:256]


def cross_kernel(n_lat, n_lon, got_ref, send_ref):
    cross = jnp.zeros((2, 128), F32)
    for i in range(n_lat - 1):
        cross = cross + got_ref[i, 2:4, :] * got_ref[i + 1, 0:2, :]
    cross = jnp.sum(jnp.sum(cross, axis=0, keepdims=True), axis=1, keepdims=True)
    small = iota((1, 128), 1)
    total = jnp.where(small < 2, jnp.sum(got_ref[:, 0:1, :], axis=0), 0.0) - jnp.where(small == 1, 2.0 * cross, 0.0)
    for p in range(n_lon):
        send_ref[p] = total


def final_kernel(n_lat, z_ref, image_ref, rhs_ref, ocean_ref, got_ref, sums_ref, sol_ref, res_ref, pre_ref):
    me = lax.axis_index("lat")
    row = iota((ROWS, EXT), 0)
    z = z_ref[...]
    sums = jnp.sum(sums_ref[...], axis=0)
    small = iota((1, 128), 1)
    affinity = jnp.sum(jnp.where(small == 0, sums, 0.0), axis=1, keepdims=True)
    energy = jnp.sum(jnp.where(small == 1, sums, 0.0), axis=1, keepdims=True)
    alpha = affinity / energy

    def line(index, first, inside):
        face = jnp.concatenate([got_ref[index, first : first + 1, :], got_ref[index, first + 1 : first + 2, :]], axis=1)
        return jnp.where(inside, face, 0.0)

    z_north = line(jnp.maximum(me - 1, 0), 2, me > 0)
    z_south = line(jnp.minimum(me + 1, n_lat - 1), 0, me < n_lat - 1)
    edge = jnp.where(row == 0, z_north, jnp.where(row == ROWS - 1, z_south, 0.0))
    image = image_ref[...] - ocean_ref[...] * edge

    def store(ref, x):
        ref[...] = jnp.transpose(x)[HW : HW + COLS, :]

    store(pre_ref, z)
    store(sol_ref, alpha * z)
    store(res_ref, rhs_ref[...] - alpha * image)


def body(land_sea, obs_cell, obs_value, obs_weight, intersection, factors, coarse_inverse):
    n_lat, n_lon = lax.axis_size("lat"), lax.axis_size("lon")
    n_row = n_lat * 16 // 128
    ring = [(j, (j + 1) % n_lon) for j in range(n_lon)]
    back = [(b, a) for a, b in ring]
    line = [(i, i + 1) for i in range(n_lat - 1)]
    up = [(b, a) for a, b in line]
    tile = (ROWS, EXT)

    def k(kernel, *static):
        def run(*refs):
            kernel(*static, *refs)

        run.__name__ = kernel.__name__
        return run

    slab = (TRI, EXT)
    more = 32 + 4 * coarse_inverse.shape[1] // EXT
    to_s, to_n, diag, rhs, ocean, send, extra = call(
        k(first_kernel, n_lat),
        [slab, slab, tile, tile, tile, (n_lat, 2, 128), (2, more, EXT)],
        (
            intersection,
            *(
                pltpu.with_memory_space_constraint(x, pltpu.HBM)
                for x in (
                    factors,
                    land_sea.T,
                    obs_cell.reshape(1, OBS),
                    obs_value.reshape(1, OBS),
                    obs_weight.reshape(1, OBS),
                    coarse_inverse,
                )
            ),
        ),
        places="shhhhhh",
        limit=16384,
        scratch=[
            pltpu.VMEM((16, 16, EXT), F32),
            pltpu.VMEM((16, 16, EXT), F32),
            pltpu.VMEM((EXT, ROWS), jnp.int32),
            pltpu.VMEM((1, OBS), jnp.int32),
            pltpu.VMEM((1, OBS), F32),
            pltpu.VMEM((1, OBS), F32),
            pltpu.VMEM((6 * ROWS, OBS), jnp.bfloat16),
            pltpu.VMEM((EXT, OBS), jnp.bfloat16),
            pltpu.VMEM(coarse_inverse.shape, F32),
            pltpu.SemaphoreType.DMA((7,)),
        ],
    )
    from_n = lax.ppermute(to_s, "lat", line)
    from_s = lax.ppermute(to_n, "lat", up)
    got = lax.all_to_all(send, "lat", 0, 0, tiled=True)
    message = (TRI + more, EXT)
    to_e, to_w, send = call(
        k(side_kernel, n_lon, n_row),
        [message, message, (n_lon, n_row, 128)],
        (intersection, factors, from_n, from_s, extra, got),
        places="svvvvv",
    )
    from_w = lax.ppermute(to_e, "lon", ring)
    from_e = lax.ppermute(to_w, "lon", back)
    coarse = lax.all_to_all(send, "lon", 0, 0, tiled=True)
    z, image, send = call(
        k(solve_kernel, n_lat, n_lon, n_row),
        [tile, tile, (n_lat, 4, 128)],
        (factors, rhs, ocean, diag, to_w, to_e, from_w, from_e, from_n, from_s, coarse_inverse, got, coarse),
        scratch=[pltpu.VMEM(tile, F32), pltpu.VMEM(tile, F32), pltpu.VMEM(tile, F32)],
    )
    edges = lax.all_to_all(send, "lat", 0, 0, tiled=True)
    (send,) = call(k(cross_kernel, n_lat, n_lon), [(n_lon, 1, 128)], (edges,))
    sums = lax.all_to_all(send, "lon", 0, 0, tiled=True)
    out = (COLS, ROWS)
    return tuple(
        x.T for x in call(k(final_kernel, n_lat), [out, out, out], (z, image, rhs, ocean, edges, sums))
    )


def solution(mesh):
    in_specs = (
        P("lat", "lon"),
        P("lat", "lon", None),
        P("lat", "lon", None),
        P("lat", "lon", None),
        P("lat", "lon"),
        P("lat", None, None, "lon"),
        P(("lon", "lat"), None),
    )
    out_specs = (P("lat", "lon"), P("lat", "lon"), P("lat", "lon"))
    return jax.shard_map(body, mesh=mesh, in_specs=in_specs, out_specs=out_specs, check_vma=False)
```

```python
import jax
import jax.numpy as jnp
from jax import lax
from jax.experimental import pallas as pl
from jax.experimental.pallas import tpu as pltpu
from jax.sharding import PartitionSpec as P

F32 = jnp.float32
DAMPING = 0.02
ROWS, COLS, HW, EXT = 128, 224, 16, 256
BLK = 8
TRI = 192
OBS = 2048
RING = ([170] + [144 + 16 * k for k in range(1, 7)] + [171], [255, 170, 171] + [127 + 16 * k for k in range(3, 8)])

VM = pl.BlockSpec(memory_space=pltpu.VMEM)
PLACES = {
    "v": VM,
    "s": pl.BlockSpec(memory_space=pltpu.SMEM),
    "h": pl.BlockSpec(memory_space=pltpu.HBM),
}


def iota(shape, dim):
    return lax.broadcasted_iota(jnp.int32, shape, dim)


def call(kernel, outs, ins, scratch=(), flops=100000, limit=16384, places=None, out=VM):
    size = sum(4 * x.size for x in ins)
    return pl.pallas_call(
        kernel,
        out_shape=[jax.ShapeDtypeStruct(s, F32) for s in outs],
        in_specs=[PLACES[p] for p in places or "v" * len(ins)],
        out_specs=[out] * len(outs),
        scratch_shapes=list(scratch),
        cost_estimate=pl.CostEstimate(flops=flops, bytes_accessed=size, transcendentals=0),
        compiler_params=pltpu.CompilerParams(vmem_limit_bytes=limit << 10),
    )(*ins)


def tri_rows(get):
    return jnp.concatenate([get(p, 8) for p in range(8)] + [get(p, 16) for p in range(8, 16)], axis=0)


def pieces(x):
    hi = x.astype(jnp.bfloat16).astype(F32)
    rest = x - hi
    mid = rest.astype(jnp.bfloat16).astype(F32)
    low = (rest - mid).astype(jnp.bfloat16).astype(F32)
    return hi, mid, low


def first_kernel(n_lat, reach_ref, fac_hbm, land_hbm, cell_hbm, value_hbm, weight_hbm, inverse_hbm, south_ref, north_ref, diag_ref,
                 rhs_ref, ocean_ref, send_ref, extra_ref, first, last, wide, cell_ref, value_ref, weight_ref, left, right,
                 inverse_ref, sems):
    moves = (
        (cell_hbm, cell_ref),
        (value_hbm, value_ref),
        (weight_hbm, weight_ref),
        (land_hbm, wide.at[pl.ds(HW, COLS), :]),
        (fac_hbm.at[0], first),
        (fac_hbm.at[BLK + 1], last),
        (inverse_hbm, inverse_ref),
    )
    copies = [pltpu.make_async_copy(src, dst, sems.at[n]) for n, (src, dst) in enumerate(moves)]
    for copy in copies:
        copy.start()
    me = lax.axis_index("lat")
    wide[0:HW, :] = jnp.zeros((HW, ROWS), jnp.int32)
    wide[HW + COLS : EXT, :] = jnp.zeros((HW, ROWS), jnp.int32)
    for copy in copies[:4]:
        copy.wait()
    ocean = jnp.transpose(wide[...].astype(F32))
    ocean_ref[...] = ocean
    step = 512
    for start in range(0, OBS, step):
        cut = slice(start, start + step)
        cell = cell_ref[:, cut]
        at_row = ((cell >> 5) * 9363) >> 16
        at_col = cell - at_row * COLS + HW
        weight = weight_ref[:, cut]
        parts = pieces(weight) + pieces(weight * value_ref[:, cut])
        hit = iota((ROWS, step), 0) == at_row
        for n, part in enumerate(parts):
            left[n * ROWS : (n + 1) * ROWS, cut] = jnp.where(hit, part, 0.0).astype(jnp.bfloat16)
        right[:, cut] = jnp.where(iota((EXT, step), 0) == at_col, 1.0, 0.0).astype(jnp.bfloat16)
    sums = lax.dot_general(left[...], right[...], (((1,), (1,)), ((), ())), preferred_element_type=F32)
    part = [sums[n * ROWS : (n + 1) * ROWS] for n in range(6)]
    diag_ref[...] = part[0] + (part[1] + part[2])
    rhs = ocean * (part[3] + (part[4] + part[5]))
    rhs_ref[...] = rhs
    sub = iota((16, EXT), 0)
    lane = iota((16, EXT), 1)
    pooled = jnp.zeros((16, EXT), F32)
    for s in range(4):
        band = jnp.sum(rhs[s * 32 : s * 32 + 32], axis=0, keepdims=True)
        pooled = jnp.where((sub >> 2) == s, band, pooled)
    begin = HW + (sub & 3) * 56
    pooled = jnp.where((lane >= begin) & (lane < begin + 56), pooled, 0.0)
    coarse = jnp.sum(pooled, axis=1, keepdims=True)
    spare = jnp.sum(jnp.where(lane == sub, coarse, 0.0), axis=0, keepdims=True)
    edge_lane = iota((1, EXT), 1)
    for p in range(n_lat):
        face = jnp.where(edge_lane < HW, spare, jnp.where(p < me, ocean[0:1], ocean[ROWS - 1 : ROWS]))
        send_ref[p, 0:1, :] = face[:, 0:128]
        send_ref[p, 1:2, :] = face[:, 128:256]
    for copy in copies[4:6]:
        copy.wait()
    edge = iota((TRI, EXT), 1)
    row = iota((TRI, EXT), 0)
    q = jnp.where(row < 64, row & 7, row & 15)
    reach = reach_ref[0, 0]
    inside = (edge >= HW - reach) & (edge < HW + COLS + reach)
    north_ref[...] = jnp.where(inside & (q >= HW - reach), tri_rows(lambda p, n: first[p, 0:n, :]), 0.0)
    south_ref[...] = jnp.where(inside & (q < reach), tri_rows(lambda p, n: last[p, 0:n, :]), 0.0)
    side_lane = iota((16, EXT), 1)
    for half, face, edge in ((0, 16, 0), (1, 239, 15)):
        load = jnp.zeros((16, EXT), F32)
        mask = jnp.zeros((16, EXT), F32)
        for k in range(BLK):
            spots = (side_lane == k * 16 + edge) | (side_lane == RING[half][k])
            if k == 0:
                spots = spots | (side_lane == 128 + edge) | (side_lane == 168)
            if k == BLK - 1:
                spots = spots | (side_lane == 144 + edge) | (side_lane == 169)
            load = jnp.where(spots, rhs[k * 16 : k * 16 + 16, face : face + 1], load)
            mask = jnp.where(spots, ocean[k * 16 : k * 16 + 16, face : face + 1], mask)
        extra_ref[half, 0:16, :] = load
        extra_ref[half, 16:32, :] = mask
    copies[6].wait()
    for half in range(2):
        for m in range(inverse_ref.shape[1] // EXT):
            for t in range(4):
                at_row, source = 32 + 4 * m + t, 4 * t + 3 * half
                extra_ref[half, at_row : at_row + 1, :] = inverse_ref[source : source + 1, m * EXT : (m + 1) * EXT]


def side_kernel(n_lon, n_row, reach_ref, fac_ref, from_n_ref, from_s_ref, extra_ref, got_ref, to_e_ref,
                to_w_ref, send_ref):
    reach = reach_ref[0, 0]
    lane = iota((TRI, 128), 1)
    for ref, half, face, start in ((to_e_ref, 1, 111, 112), (to_w_ref, 0, 16, 0)):
        lanes = slice(half * 128, half * 128 + 128)
        bulk = jnp.zeros((TRI, 128), F32)
        rest = jnp.zeros((TRI, 128), F32)
        for k in range(BLK):
            block = tri_rows(lambda p, n: fac_ref[k + 1, p, 0:n, lanes])
            at = lane - k * 16
            own = (at >= 0) & (at < jnp.minimum(reach, 16)) if half else (at >= HW - reach) & (at < 16)
            shift = (k * 16 - start) % 128
            moved = pltpu.roll(block, shift, 1) if shift else block
            bulk = jnp.where(own, moved, bulk)
            ring = RING[half][k] - 128
            if (face + shift) % 128 != ring:
                moved = pltpu.roll(block, (ring - face) % 128, 1)
            rest = jnp.where(lane == ring, moved, rest)
        north, south = from_n_ref[:, lanes], from_s_ref[:, lanes]
        rest = jnp.where(lane < 16, pltpu.roll(north, 16, 1) if half else north, rest)
        rest = jnp.where((lane >= 16) & (lane < 32), pltpu.roll(south, 32 if half else 16, 1), rest)
        rest = jnp.where(lane == 40, pltpu.roll(north, (40 - face) % 128, 1), rest)
        rest = jnp.where(lane == 41, pltpu.roll(south, (41 - face) % 128, 1), rest)
        ref[0:TRI, 0:128] = bulk
        ref[0:TRI, 128:256] = rest
        ref[TRI:, :] = extra_ref[half]
    small = iota((1, 128), 1)
    total = [jnp.zeros((1, 128), F32) for _ in range(n_row)]
    for p in range(n_row * 8):
        at = p * 16 % 128
        part = pltpu.roll(got_ref[p, 0:1, :], at, 1) if at else got_ref[p, 0:1, :]
        total[p // 8] = jnp.where((small >= at) & (small < at + 16), part, total[p // 8])
    for p in range(n_lon):
        for r in range(n_row):
            send_ref[p, r : r + 1, :] = total[r]


def apply_block(u, get):
    low = u[0:8]
    g_low = jnp.zeros_like(low)
    g_high = jnp.zeros_like(low)
    for p in range(8):
        line = get(p, 8)
        f = jnp.sum(line * low, axis=0, keepdims=True)
        g_low = g_low + line * f
    for p in range(8, 16):
        line = get(p, 16)
        f = jnp.sum(line * u, axis=0, keepdims=True)
        g = line * f
        g_low = g_low + g[0:8]
        g_high = g_high + g[8:16]
    return jnp.concatenate([g_low, g_high], axis=0)


def tri_get(ref):
    def get(p, n):
        start = p * 8 if p < 8 else 64 + (p - 8) * 16
        return ref[start : start + n, :]

    return get


def solve_kernel(n_lat, n_lon, n_row, fac_ref, rhs_ref, ocean_ref, diag_ref, to_w_ref, to_e_ref, from_w_ref, from_e_ref,
                 from_n_ref, from_s_ref, inverse_ref, got_ref, coarse_ref, z_ref, image_ref, send_ref, acc, z_pad, o_pad):
    me = lax.axis_index("lat")
    lane = iota((16, 128), 1)
    wide_lane = iota((16, EXT), 1)
    u_w = jnp.zeros((16, 128), F32)
    u_e = jnp.zeros((16, 128), F32)
    for k in range(BLK):
        rows = slice(k * 16, k * 16 + 16)
        u = rhs_ref[rows, :]
        acc[rows, :] = apply_block(u, lambda p, n: fac_ref[k + 1, p, 0:n, :])
        own = (lane >= k * 16) & (lane < k * 16 + 16)
        u_w = jnp.where(own, pltpu.roll(u[:, 0:128], (k * 16 - 16) % 128, 1), u_w)
        u_e = jnp.where(own, pltpu.roll(u[:, 128:256], (k * 16 - 96) % 128, 1), u_e)
    top, end = rhs_ref[0:16, :], rhs_ref[ROWS - 16 : ROWS, :]

    def corners(top, end, at):
        return jnp.where(
            lane < 16, pltpu.roll(top, (-at) % 128, 1), jnp.where(lane < 32, pltpu.roll(end, (16 - at) % 128, 1), 0.0)
        )

    ring_w, ring_e = from_w_ref[TRI : TRI + 16, :], from_e_ref[TRI : TRI + 16, :]
    u_w = jnp.concatenate([u_w, corners(top[:, 0:128], end[:, 0:128], 16)], axis=1)
    u_e = jnp.concatenate([u_e, corners(top[:, 128:256], end[:, 128:256], 96)], axis=1)
    u_w = jnp.where(wide_lane >= 160, ring_w, u_w)
    u_e = jnp.where(wide_lane >= 160, ring_e, u_e)
    g_w = apply_block(u_w, tri_get(from_w_ref))
    g_e = apply_block(u_e, tri_get(from_e_ref))
    own_w, own_e = tri_get(to_w_ref), tri_get(to_e_ref)

    def own_get(p, n):
        return jnp.where((wide_lane[0:n] & 15) == 0, own_e(p, n), own_w(p, n))

    h = apply_block(jnp.where((wide_lane & 15) == 0, ring_e, ring_w), own_get)
    in_w = (lane >= 16) & (lane < 32)
    in_e = (lane >= 96) & (lane < 112)
    for k in range(BLK):
        rows = slice(k * 16, k * 16 + 16)
        add_w = pltpu.roll(g_w[:, 0:128], (16 - k * 16) % 128, 1)
        add_e = pltpu.roll(g_e[:, 0:128], (96 - k * 16) % 128, 1)
        if k == 0:
            add_w = add_w + pltpu.roll(g_w[:, 128:256], 16, 1)
            add_e = add_e + pltpu.roll(g_e[:, 128:256], 96, 1)
        if k == BLK - 1:
            add_w = add_w + g_w[:, 128:256]
            add_e = add_e + pltpu.roll(g_e[:, 128:256], 80, 1)
        acc[rows, 0:128] += jnp.where(in_w, add_w, 0.0)
        acc[rows, 128:256] += jnp.where(in_e, add_e, 0.0)
    for rows, ref in ((slice(0, 16), from_n_ref), (slice(ROWS - 16, ROWS), from_s_ref)):
        acc[rows, :] += apply_block(rhs_ref[rows, :], tri_get(ref))
    dot = jnp.zeros((16, EXT), F32)
    dot_w = jnp.zeros((4, EXT), F32)
    dot_e = jnp.zeros((4, EXT), F32)
    for m in range(n_lon * n_row // 2):
        part = [coarse_ref[n // n_row, n % n_row : n % n_row + 1, :] for n in (2 * m, 2 * m + 1)]
        part = jnp.concatenate(part, axis=1)
        dot = dot + inverse_ref[:, m * EXT : (m + 1) * EXT] * part
        at_row = TRI + 32 + 4 * m
        dot_w = dot_w + from_w_ref[at_row : at_row + 4, :] * part
        dot_e = dot_e + from_e_ref[at_row : at_row + 4, :] * part
    answer = jnp.sum(dot, axis=1, keepdims=True)
    answer_w = jnp.sum(dot_w, axis=1, keepdims=True)
    answer_e = jnp.sum(dot_e, axis=1, keepdims=True)
    sub = iota((16, EXT), 0)
    first = HW + (sub & 3) * 56
    spread = jnp.where((wide_lane >= first) & (wide_lane < first + 56), answer, 0.0)
    for k in range(BLK):
        rows = slice(k * 16, k * 16 + 16)
        s = k // 2
        band = jnp.sum(jnp.where((sub >> 2) == s, spread, 0.0), axis=0, keepdims=True)
        ocean = ocean_ref[rows, :]
        z = ocean * (acc[rows, :] + band)
        z_ref[rows, :] = z

        def edge(g, ref, at, spot, answer):
            ring = h[:, k * 16 + at : k * 16 + at + 1] + g[:, spot : spot + 1]
            if k == 0:
                ring = ring + (h[:, 128 + at : 129 + at] + g[:, 168:169])
            if k == BLK - 1:
                ring = ring + (h[:, 144 + at : 145 + at] + g[:, 169:170])
            mask = ref[TRI + 16 : TRI + 32, spot : spot + 1]
            return mask, mask * (ring + answer[s : s + 1])

        o_w, z_w = edge(g_w, from_w_ref, 15, RING[1][k], answer_w)
        o_e, z_e = edge(g_e, from_e_ref, 0, RING[0][k], answer_e)
        z_pad[rows, :] = jnp.where(wide_lane == 15, z_w, jnp.where(wide_lane == 240, z_e, z))
        o_pad[rows, :] = jnp.where(wide_lane == 15, o_w, jnp.where(wide_lane == 240, o_e, ocean))

    row = iota((ROWS, EXT), 0)
    z = z_ref[...]
    ocean = ocean_ref[...]

    def sides(x):
        return pltpu.roll(x, 1, 1) + pltpu.roll(x, EXT - 1, 1)

    def line(index, inside):
        face = jnp.concatenate([got_ref[index, 0:1, :], got_ref[index, 1:2, :]], axis=1)
        return jnp.where(inside & (iota((1, EXT), 1) >= HW), face, 0.0)

    o_north = line(jnp.maximum(me - 1, 0), me > 0)
    o_south = line(jnp.minimum(me + 1, n_lat - 1), me < n_lat - 1)

    def rows(x, north, south):
        return jnp.where(row == 0, north, pltpu.roll(x, 1, 0)) + jnp.where(
            row == ROWS - 1, south, pltpu.roll(x, ROWS - 1, 0)
        )

    total = sides(o_pad[...]) + rows(ocean, o_north, o_south)
    beside = sides(z_pad[...]) + rows(z, 0.0, 0.0)
    image = ocean * ((diag_ref[...] + DAMPING) * z + (total * z - beside)) + (1.0 - ocean) * z
    image_ref[...] = image
    affinity = jnp.sum(jnp.sum(rhs_ref[...] * z, axis=0, keepdims=True), axis=1, keepdims=True)
    energy = jnp.sum(jnp.sum(z * image, axis=0, keepdims=True), axis=1, keepdims=True)
    small = iota((1, 128), 1)
    scalars = jnp.where(small == 0, affinity, jnp.where(small == 1, energy, 0.0))
    for p in range(n_lat):
        send_ref[p, 0:1, :] = jnp.where(small < 2, scalars, z[0:1, 0:128])
        send_ref[p, 1:2, :] = z[0:1, 128:256]
        send_ref[p, 2:3, :] = z[ROWS - 1 : ROWS, 0:128]
        send_ref[p, 3:4, :] = z[ROWS - 1 : ROWS, 128:256]


def cross_kernel(n_lat, n_lon, got_ref, send_ref):
    cross = jnp.zeros((2, 128), F32)
    for i in range(n_lat - 1):
        cross = cross + got_ref[i, 2:4, :] * got_ref[i + 1, 0:2, :]
    cross = jnp.sum(jnp.sum(cross, axis=0, keepdims=True), axis=1, keepdims=True)
    small = iota((1, 128), 1)
    total = jnp.where(small < 2, jnp.sum(got_ref[:, 0:1, :], axis=0), 0.0) - jnp.where(small == 1, 2.0 * cross, 0.0)
    for p in range(n_lon):
        send_ref[p] = total


def final_kernel(n_lat, z_ref, image_ref, rhs_ref, ocean_ref, got_ref, sums_ref, sol_hbm, res_hbm, pre_hbm, sol_ref, res_ref,
                 pre_ref, sems):
    def store(n, ref, hbm, x):
        ref[...] = jnp.transpose(x)[HW : HW + COLS, :]
        copy = pltpu.make_async_copy(ref, hbm, sems.at[n])
        copy.start()
        return copy

    me = lax.axis_index("lat")
    row = iota((ROWS, EXT), 0)
    z = z_ref[...]
    copies = [store(0, pre_ref, pre_hbm, z)]
    sums = jnp.sum(sums_ref[...], axis=0)
    small = iota((1, 128), 1)
    affinity = jnp.sum(jnp.where(small == 0, sums, 0.0), axis=1, keepdims=True)
    energy = jnp.sum(jnp.where(small == 1, sums, 0.0), axis=1, keepdims=True)
    alpha = affinity / energy

    def line(index, first, inside):
        face = jnp.concatenate([got_ref[index, first : first + 1, :], got_ref[index, first + 1 : first + 2, :]], axis=1)
        return jnp.where(inside, face, 0.0)

    z_north = line(jnp.maximum(me - 1, 0), 2, me > 0)
    z_south = line(jnp.minimum(me + 1, n_lat - 1), 0, me < n_lat - 1)
    edge = jnp.where(row == 0, z_north, jnp.where(row == ROWS - 1, z_south, 0.0))
    image = image_ref[...] - ocean_ref[...] * edge

    copies.append(store(1, sol_ref, sol_hbm, alpha * z))
    copies.append(store(2, res_ref, res_hbm, rhs_ref[...] - alpha * image))
    for copy in copies:
        copy.wait()


def body(land_sea, obs_cell, obs_value, obs_weight, intersection, factors, coarse_inverse):
    n_lat, n_lon = lax.axis_size("lat"), lax.axis_size("lon")
    n_row = n_lat * 16 // 128
    ring = [(j, (j + 1) % n_lon) for j in range(n_lon)]
    back = [(b, a) for a, b in ring]
    line = [(i, i + 1) for i in range(n_lat - 1)]
    up = [(b, a) for a, b in line]
    tile = (ROWS, EXT)

    def k(kernel, *static):
        def run(*refs):
            kernel(*static, *refs)

        run.__name__ = kernel.__name__
        return run

    slab = (TRI, EXT)
    more = 32 + 4 * coarse_inverse.shape[1] // EXT
    to_s, to_n, diag, rhs, ocean, send, extra = call(
        k(first_kernel, n_lat),
        [slab, slab, tile, tile, tile, (n_lat, 2, 128), (2, more, EXT)],
        (
            intersection,
            *(
                pltpu.with_memory_space_constraint(x, pltpu.HBM)
                for x in (
                    factors,
                    land_sea.T,
                    obs_cell.reshape(1, OBS),
                    obs_value.reshape(1, OBS),
                    obs_weight.reshape(1, OBS),
                    coarse_inverse,
                )
            ),
        ),
        places="shhhhhh",
        limit=16384,
        scratch=[
            pltpu.VMEM((16, 16, EXT), F32),
            pltpu.VMEM((16, 16, EXT), F32),
            pltpu.VMEM((EXT, ROWS), jnp.int32),
            pltpu.VMEM((1, OBS), jnp.int32),
            pltpu.VMEM((1, OBS), F32),
            pltpu.VMEM((1, OBS), F32),
            pltpu.VMEM((6 * ROWS, OBS), jnp.bfloat16),
            pltpu.VMEM((EXT, OBS), jnp.bfloat16),
            pltpu.VMEM(coarse_inverse.shape, F32),
            pltpu.SemaphoreType.DMA((7,)),
        ],
    )
    from_n = lax.ppermute(to_s, "lat", line)
    from_s = lax.ppermute(to_n, "lat", up)
    got = lax.all_to_all(send, "lat", 0, 0, tiled=True)
    message = (TRI + more, EXT)
    to_e, to_w, send = call(
        k(side_kernel, n_lon, n_row),
        [message, message, (n_lon, n_row, 128)],
        (intersection, factors, from_n, from_s, extra, got),
        places="svvvvv",
    )
    from_w = lax.ppermute(to_e, "lon", ring)
    from_e = lax.ppermute(to_w, "lon", back)
    coarse = lax.all_to_all(send, "lon", 0, 0, tiled=True)
    z, image, send = call(
        k(solve_kernel, n_lat, n_lon, n_row),
        [tile, tile, (n_lat, 4, 128)],
        (factors, rhs, ocean, diag, to_w, to_e, from_w, from_e, from_n, from_s, coarse_inverse, got, coarse),
        scratch=[pltpu.VMEM(tile, F32), pltpu.VMEM(tile, F32), pltpu.VMEM(tile, F32)],
    )
    edges = lax.all_to_all(send, "lat", 0, 0, tiled=True)
    (send,) = call(k(cross_kernel, n_lat, n_lon), [(n_lon, 1, 128)], (edges,))
    sums = lax.all_to_all(send, "lon", 0, 0, tiled=True)
    out = (COLS, ROWS)
    outs = call(
        k(final_kernel, n_lat),
        [out, out, out],
        (z, image, rhs, ocean, edges, sums),
        scratch=[pltpu.VMEM(out, F32)] * 3 + [pltpu.SemaphoreType.DMA((3,))],
        out=PLACES["h"],
    )
    return tuple(x.T for x in outs)


def solution(mesh):
    in_specs = (
        P("lat", "lon"),
        P("lat", "lon", None),
        P("lat", "lon", None),
        P("lat", "lon", None),
        P("lat", "lon"),
        P("lat", None, None, "lon"),
        P(("lon", "lat"), None),
    )
    out_specs = (P("lat", "lon"), P("lat", "lon"), P("lat", "lon"))
    return jax.shard_map(body, mesh=mesh, in_specs=in_specs, out_specs=out_specs, check_vma=False)
```
